768 devices in a mesh: mp: 48 (over z_hi, y, core), ens: 16 (over x, z_lo).
Axes of the slice: x: 4, y: 8, z: 12 (z_hi: 3, z_lo: 4; z = z_hi * 4 + z_lo), core: 2. Of those that a mesh axis runs over, the one named last changes fastest.
Arguments:
- ensemble: bfloat16 [192, 16, 16, 288], P('mp', 'ens'), may hold values from -1 to 1
- control: bfloat16 [192, 16, 16, 288], P(None, 'ens', None, 'mp'), may hold values from -6 to 6
- band: int32 [192], replicated, may hold values from 4 to 32
- wind_east: bfloat16 [192, 16, 288], P('mp'), may hold values from -0.44921875 to 0.44921875
- wind_north: bfloat16 [192, 16, 288], P('mp'), may hold values from -0.44921875 to 0.44921875
- observation_longitude: int32 [4, 192, 128], P(None, 'mp'), may hold values from 0 to 287
- innovation: float32 [4, 192, 16, 128], P(None, 'mp'), may hold values from -6 to 6
- observation_weight: float32 [4, 192, 128], P(None, 'mp'), may hold values from 0.25 to 4
Outputs:
- gradient: float32 [192, 16, 16, 288], P(None, 'ens', None, 'mp')
- departures: float32 [4, 192, 16, 128], P(None, 'mp', 'ens')
The draws below stay inside these ranges and needn't reach their ends.
All inputs are finite; a program needn't handle non-finite values.
Results may differ from the reference program's by a relative error of at most 0.0027.
Values may be sent and summed in bfloat16 or wider, within the bound.
A program may use at most 32 MiB of HBM per device.

```python
import math
import jax
import jax.numpy as jnp

LAT_DEV = 4
VERTICAL_LEVELS = 16
TIME_SLOTS = 4
OBSERVATION_COUNT = 128
LATITUDE_ROWS = 192
LONGITUDE_COUNT = 288
MEM = 16


def set_ends(values, stream_key, low, high):
    place = [jax.random.randint(jax.random.fold_in(stream_key, axis), (), 0, length) for axis, length in enumerate(values.shape)]
    longest = values.shape.index(max(values.shape))
    neighbour = place[:longest] + [(place[longest] + 1) % values.shape[longest]] + place[longest + 1:]
    return values.at[tuple(place)].set(low).at[tuple(neighbour)].set(high)


def block_scale(own_key, shape, shards, smallest, high):
    def one(dim, blocks):
        steps = jax.random.uniform(jax.random.fold_in(jax.random.fold_in(own_key, 6), dim), (blocks,), jnp.float32, smallest / len(shards), high / len(shards))
        return jnp.repeat(jnp.exp(steps), shape[dim] // blocks).reshape((-1,) + (1,) * (len(shape) - dim - 1))

    factor_of = one(*shards[0])
    for cut in shards[1:]:
        factor_of = factor_of * one(*cut)
    return factor_of


def scatter_about(stream_key, dims, width, limit, pieces=(), kind=jnp.bfloat16):
    gain = block_scale(stream_key, dims, pieces, -0.22, 0.18) if pieces else 1.0
    values = jax.random.normal(stream_key, dims, jnp.float32) * width * gain
    return jnp.minimum(jnp.maximum(values, -limit), limit).astype(kind)


def setup_inputs(seed: int = 0) -> dict:
    key_of = jax.random.split(jax.random.key(seed), 9)
    ensemble = scatter_about(key_of[0], (LATITUDE_ROWS, MEM, VERTICAL_LEVELS, LONGITUDE_COUNT), (0.3 * MEM ** -0.5), 1.0, ((0, 48), (1, 16)))
    control = scatter_about(key_of[1], (LATITUDE_ROWS, MEM, VERTICAL_LEVELS, LONGITUDE_COUNT), 1.0, 6.0, ((1, 16), (3, 48)))
    band = set_ends(jax.random.randint(key_of[2], (LATITUDE_ROWS,), LAT_DEV, 8 * LAT_DEV + 1), jax.random.fold_in(key_of[2], 1), LAT_DEV, 8 * LAT_DEV).astype(jnp.int32)
    wind_east = jnp.clip(jax.random.uniform(key_of[3], (LATITUDE_ROWS, VERTICAL_LEVELS, LONGITUDE_COUNT), jnp.float32, -0.44921875, 0.44921875) * block_scale(key_of[3], (LATITUDE_ROWS, VERTICAL_LEVELS, LONGITUDE_COUNT), ((0, 48),), -0.4, 0.0), -0.44921875, 0.44921875).astype(jnp.bfloat16)
    wind_north = jnp.clip(jax.random.uniform(key_of[4], (LATITUDE_ROWS, VERTICAL_LEVELS, LONGITUDE_COUNT), jnp.float32, -0.44921875, 0.44921875) * block_scale(key_of[4], (LATITUDE_ROWS, VERTICAL_LEVELS, LONGITUDE_COUNT), ((0, 48),), -0.4, 0.0), -0.44921875, 0.44921875).astype(jnp.bfloat16)
    observation_longitude = set_ends(jax.random.randint(key_of[5], (TIME_SLOTS, LATITUDE_ROWS, OBSERVATION_COUNT), 0, LONGITUDE_COUNT), jax.random.fold_in(key_of[5], 1), 0, LONGITUDE_COUNT - 1).astype(jnp.int32)
    innovation = scatter_about(key_of[6], (TIME_SLOTS, LATITUDE_ROWS, VERTICAL_LEVELS, OBSERVATION_COUNT), 1.0, 6.0, ((1, 48),), jnp.float32)
    observation_weight = jnp.clip(jnp.exp(math.log(4.0) - 2.7725887 * jax.random.uniform(key_of[7], (TIME_SLOTS, LATITUDE_ROWS, OBSERVATION_COUNT), jnp.float32) ** block_scale(key_of[7], (TIME_SLOTS, LATITUDE_ROWS, OBSERVATION_COUNT), ((1, 48),), -0.2, 0.2)), 0.25, 4.0)
    return {"ensemble": ensemble, "control": control, "band": band, "wind_east": wind_east, "wind_north": wind_north, "observation_longitude": observation_longitude, "innovation": innovation, "observation_weight": observation_weight}


def localization(band):
    row_count = band.shape[0]
    latitude = jnp.arange(row_count, dtype=jnp.float32)
    widths = band.astype(jnp.float32)
    distance = jnp.abs(latitude[:, None] - latitude[None, :])
    return jnp.maximum(0.0, 1.0 - 2.0 * distance / (widths[:, None] + widths[None, :])).astype(jnp.bfloat16)


def apply_rows(kernel, quantity):
    shaped = quantity.reshape(quantity.shape[0], -1)
    return jnp.dot(kernel, shaped, preferred_element_type=jnp.float32).reshape(quantity.shape)


def coefficients(wind_east, wind_north):
    east_rate = wind_east.astype(jnp.float32)
    north_rate = wind_north.astype(jnp.float32)
    return (1.0 - jnp.abs(east_rate) - jnp.abs(north_rate), jnp.maximum(east_rate, 0.0), jnp.maximum(-east_rate, 0.0), jnp.maximum(north_rate, 0.0), jnp.maximum(-north_rate, 0.0))


def below(quantity):
    zero_row = jnp.zeros_like(quantity[:1])
    return jnp.concatenate([zero_row, quantity[:-1]], axis=0)


def above(quantity):
    zero_row = jnp.zeros_like(quantity[:1])
    return jnp.concatenate([quantity[1:], zero_row], axis=0)


def forward(quantity, coeffs):
    center, from_west, from_east, from_south, from_north = coeffs
    result = center * quantity + from_west * jnp.roll(quantity, 1, axis=2) + from_east * jnp.roll(quantity, -1, axis=2)
    return result + from_south * below(quantity) + from_north * above(quantity)


def adjoint(quantity, coeffs):
    center, from_west, from_east, from_south, from_north = coeffs
    result = center * quantity + jnp.roll(from_west * quantity, -1, axis=2) + jnp.roll(from_east * quantity, 1, axis=2)
    return result + above(from_south * quantity) + below(from_north * quantity)


def sample(quantity, lon_index):
    wanted = jnp.broadcast_to(lon_index[:, None, :], (quantity.shape[0], quantity.shape[1], lon_index.shape[1]))
    return jnp.take_along_axis(quantity, wanted, axis=2)


def inject(quantity, lon_index, amounts):
    lat_index = jnp.arange(quantity.shape[0], dtype=jnp.int32)[:, None, None]
    lev_index = jnp.arange(quantity.shape[1], dtype=jnp.int32)[None, :, None]
    return quantity.at[lat_index, lev_index, lon_index[:, None, :].astype(jnp.int32)].add(amounts)


def reference(ensemble, control, band, wind_east, wind_north, observation_longitude, innovation, observation_weight):
    kernel = localization(band)
    spread = apply_rows(kernel, control).astype(jnp.bfloat16)
    increment = jnp.zeros((LATITUDE_ROWS, VERTICAL_LEVELS, LONGITUDE_COUNT), jnp.float32)
    for member in range(MEM):
        increment = increment + ensemble[:, member].astype(jnp.float32) * spread[:, member].astype(jnp.float32)
    coeffs = coefficients(wind_east, wind_north)
    quantity = increment
    departures = []
    for moment_value in range(TIME_SLOTS):
        quantity = forward(quantity, coeffs)
        departures.append(sample(quantity, observation_longitude[moment_value]) - innovation[moment_value])
    sensitivity = jnp.zeros((LATITUDE_ROWS, VERTICAL_LEVELS, LONGITUDE_COUNT), jnp.float32)
    for moment_value in reversed(range(TIME_SLOTS)):
        sensitivity = inject(sensitivity, observation_longitude[moment_value], observation_weight[moment_value][:, None, :] * departures[moment_value])
        sensitivity = adjoint(sensitivity, coeffs)
    product = (ensemble.astype(jnp.float32) * sensitivity[:, None]).astype(jnp.bfloat16)
    gradient = apply_rows(kernel, product) + control.astype(jnp.float32)
    return gradient, jnp.stack(departures)
```

```python
import functools

import jax
import jax.numpy as jnp
from jax import lax
from jax.experimental import pallas as pl
from jax.experimental.pallas import tpu as pltpu
from jax.sharding import PartitionSpec as P

MESH = pl.DeviceIdType.MESH
MP, ENS = 48, 16
LAT, LEV, LON, OBS, SLOTS = 192, 16, 288, 128, 4
TILE = 4
KB = 6
WIDE = MP * 8
ROWS = 24
F32, BF16 = jnp.float32, jnp.bfloat16


def iota(shape, dim):
    return lax.broadcasted_iota(jnp.int32, shape, dim)


def split3(value):
    first = value.astype(BF16)
    rest = value - first.astype(F32)
    second = rest.astype(BF16)
    third = (rest - second.astype(F32)).astype(BF16)
    return first.astype(F32), second.astype(F32), third.astype(F32)


def body(
    ens_hbm, ctl_hbm, band_hbm, east_hbm, north_hbm, lon_hbm, inn_hbm, wgt_hbm,
    grad_hbm, dep_hbm,
    ens_v, ctl_v, band_v, east_v, north_v, lon_v, inn_v, wgt_v, grad_v, dep_v,
    kern_v, rows_v, wide_v, ensw_v, state_v,
    a1_send, a1_recv, part_v, rs_recv, inc_v, halo_recv,
    wind_own, wind_recv, db_own, db_recv, coef_v, dfull_v, bfull_v,
    ag_send, ag_recv, a2_send, a2_recv,
    in_sem, out_sem, send_sem, recv_sem,
):
    q = lax.axis_index("mp")
    e = lax.axis_index("ens")

    pairs = [
        (ctl_hbm, ctl_v), (band_hbm, band_v), (ens_hbm, ens_v), (east_hbm, east_v),
        (north_hbm, north_v), (lon_hbm, lon_v), (inn_hbm, inn_v), (wgt_hbm, wgt_v),
    ]
    loads = [
        pltpu.make_async_copy(src, dst, in_sem.at[n]) for n, (src, dst) in enumerate(pairs)
    ]
    for copy in loads:
        copy.start()
    barrier = pltpu.get_barrier_semaphore()

    def greet_mp(d, carry):
        pl.semaphore_signal(
            barrier, inc=1, device_id={"mp": (q + d) % MP}, device_id_type=MESH
        )
        return carry

    def greet_ens(d, carry):
        pl.semaphore_signal(
            barrier, inc=1, device_id={"ens": (e + d) % ENS}, device_id_type=MESH
        )
        return carry

    lax.fori_loop(1, MP, greet_mp, 0)
    lax.fori_loop(1, ENS, greet_ens, 0)

    part_v[...] = jnp.zeros_like(part_v)
    ag_send[...] = jnp.zeros_like(ag_send)
    state_v[...] = jnp.zeros_like(state_v)
    wide_v[...] = jnp.zeros_like(wide_v)
    dfull_v[...] = jnp.zeros_like(dfull_v)
    bfull_v[...] = jnp.zeros_like(bfull_v)

    loads[1].wait()
    width_j = jnp.broadcast_to(band_v[...].astype(F32), (LAT, LAT))
    width_i = width_j.T
    distance = jnp.abs(iota((LAT, LAT), 0) - iota((LAT, LAT), 1)).astype(F32)
    kern_v[...] = jnp.maximum(0.0, 1.0 - 2.0 * distance / (width_i + width_j)).astype(BF16)

    loads[0].wait()
    spread = lax.dot_general(
        kern_v[...], ctl_v[...], (((1,), (1,)), ((), ())), preferred_element_type=F32
    )
    rows_v[...] = jnp.concatenate([spread, jnp.zeros((LAT, 128 - KB * LEV), F32)], axis=1)
    group = iota((MP, 128), 1) >> 4
    by_row = [rows_v[pl.ds(i, MP, stride=TILE), :] for i in range(TILE)]
    for k in range(KB):
        block = jnp.zeros((MP, 128), F32)
        for i in range(TILE):
            block = jnp.where(group == i, pltpu.roll(by_row[i], (16 * (i - k)) % 128, 1), block)
        wide_v[pl.ds(k, MP, stride=8), :] = block
    a1_send[...] = wide_v[...].reshape(MP, 8, 128).astype(BF16)

    pl.semaphore_wait(barrier, MP + ENS - 2)

    def send_spread(d, carry):
        to = (q + d) % MP
        pltpu.make_async_remote_copy(
            src_ref=a1_send.at[to], dst_ref=a1_recv.at[q],
            send_sem=send_sem.at[0], recv_sem=recv_sem.at[0],
            device_id={"mp": to}, device_id_type=MESH,
        ).start()
        return carry

    lax.fori_loop(1, MP, send_spread, 0)
    pltpu.make_async_copy(a1_send.at[q], a1_recv.at[q], recv_sem.at[0]).start()

    source = iota((LON, WIDE), 1)
    embed = (
        (iota((LON, WIDE), 0) == (source >> 3) * 6 + (source & 7)) & ((source & 7) < KB)
    ).astype(F32).astype(BF16)
    for copy in loads[2:5]:
        copy.wait()
    ensw_v[...] = jnp.dot(ens_v[...], embed, preferred_element_type=F32)
    mine = iota((LEV, LON), 0) == e
    winds = []
    for ref in (east_v, north_v):
        for i in range(TILE):
            level = ref[LEV * i : LEV * (i + 1), :].astype(F32)
            winds.append(jnp.sum(jnp.where(mine, level, 0.0), axis=0, keepdims=True))
    wind_own[...] = jnp.dot(
        jnp.concatenate(winds, axis=0).astype(BF16), embed, preferred_element_type=F32
    )

    offsets = (-2, -1, 1, 2)

    def to_tiles(src, dst, slots, send, recv):
        for slot, offset in slots:
            pltpu.make_async_remote_copy(
                src_ref=src, dst_ref=dst.at[slot], send_sem=send, recv_sem=recv,
                device_id={"mp": (q - offset + MP) % MP}, device_id_type=MESH,
            ).start()

    to_tiles(wind_own, wind_recv, enumerate(offsets), send_sem.at[1], recv_sem.at[1])

    for copy in loads[5:]:
        copy.wait()
    own_level = iota((LEV, OBS), 0) == e
    lane_rows = iota((WIDE, OBS), 0)
    wide_lon = []
    observed = []
    for t in range(SLOTS):
        lon = lon_v[t]
        place = lon + 2 * ((lon * 10923) >> 16)
        wide_lon.append(place)
        weight = wgt_v[t]
        level_rows = []
        for i in range(TILE):
            start = LEV * (TILE * t + i)
            level_rows.append(
                jnp.sum(
                    jnp.where(own_level, inn_v[start : start + LEV, :], 0.0),
                    axis=0, keepdims=True,
                )
            )
        level_innovation = jnp.concatenate(level_rows, axis=0)
        observed.append(level_innovation)
        parts = split3(weight) + split3(weight * level_innovation)
        for i in range(TILE):
            hits = (lane_rows == place[i : i + 1, :]).astype(F32).astype(BF16)
            lhs = jnp.concatenate(
                [part[i : i + 1, :] for part in parts] + [jnp.zeros((2, OBS), F32)], axis=0
            ).astype(BF16)
            sums = lax.dot_general(
                lhs, hits, (((1,), (1,)), ((), ())), preferred_element_type=F32
            )
            at = TILE * t + i
            db_own[at : at + 1, :] = sums[0:1] + sums[1:2] + sums[2:3]
            db_own[16 + at : 17 + at, :] = sums[3:4] + sums[4:5] + sums[5:6]
    to_tiles(db_own, db_recv, ((0, -1), (1, 1)), send_sem.at[2], recv_sem.at[2])

    pltpu.make_async_copy(a1_recv, a1_recv, recv_sem.at[0]).wait()
    native = a1_recv[...].astype(F32).reshape(WIDE, 128).T
    for i in range(TILE):
        part = ensw_v[LEV * i : LEV * (i + 1), :] * native[LEV * i : LEV * (i + 1), :]
        for c in range(3):
            part_v[pl.ds(4 * c + i, LEV, stride=16), :] = part[:, 128 * c : 128 * (c + 1)]

    def send_part(d, carry):
        to = (e + d) % ENS
        pltpu.make_async_remote_copy(
            src_ref=part_v.at[pl.ds(pl.multiple_of(to * 16, 16), 16)], dst_ref=rs_recv.at[d - 1],
            send_sem=send_sem.at[3], recv_sem=recv_sem.at[3],
            device_id={"ens": to}, device_id_type=MESH,
        ).start()
        return carry

    lax.fori_loop(1, ENS, send_part, 0)

    pltpu.make_async_copy(wind_recv, wind_recv, recv_sem.at[1]).wait()
    pltpu.make_async_copy(db_recv, db_recv, recv_sem.at[2]).wait()
    row = iota((ROWS, WIDE), 0)
    globe = row + (TILE * q - 8)
    inside = (globe >= 0) & (globe < LAT) & (row < 20)
    slabs = [wind_recv[0], wind_recv[1], wind_own[...], wind_recv[2], wind_recv[3]]
    blank = jnp.zeros((TILE, WIDE), F32)
    east = jnp.concatenate([slab[0:4] for slab in slabs] + [blank], axis=0)
    north = jnp.concatenate([slab[4:8] for slab in slabs] + [blank], axis=0)
    coefs = (
        1.0 - jnp.abs(east) - jnp.abs(north),
        jnp.maximum(east, 0.0), jnp.maximum(-east, 0.0),
        jnp.maximum(north, 0.0), jnp.maximum(-north, 0.0),
    )
    for n, coef in enumerate(coefs):
        coef_v[n] = jnp.where(inside, coef, 0.0)
    for t in range(SLOTS):
        at = TILE * t
        for full, base in ((dfull_v, 0), (bfull_v, 16)):
            full[t, 4:8, :] = db_recv[0, base + at : base + at + 4, :]
            full[t, 8:12, :] = db_own[base + at : base + at + 4, :]
            full[t, 12:16, :] = db_recv[1, base + at : base + at + 4, :]

    own_part = part_v[pl.ds(pl.multiple_of(e * 16, 16), 16), :]
    pltpu.make_async_copy(rs_recv, rs_recv, recv_sem.at[3]).wait()
    total = own_part
    for d in range(ENS - 1):
        total = total + rs_recv[d]
    inc_v[...] = total
    to_tiles(inc_v, halo_recv, enumerate(offsets), send_sem.at[4], recv_sem.at[4])
    pltpu.make_async_copy(halo_recv, halo_recv, recv_sem.at[4]).wait()
    for s in range(5):
        for c in range(3):
            if s == 2:
                piece = inc_v[4 * c : 4 * c + 4, :]
            else:
                piece = halo_recv[s if s < 2 else s - 1, 4 * c : 4 * c + 4, :]
            state_v[0, 4 * s : 4 * s + 4, 128 * c : 128 * (c + 1)] = piece

    lane = iota((ROWS, WIDE), 1) & 7
    first, last = lane == 0, lane == KB - 1

    def west(value):
        return jnp.where(first, pltpu.roll(value, 3, 1), pltpu.roll(value, 1, 1))

    def east_of(value):
        return jnp.where(last, pltpu.roll(value, WIDE - 3, 1), pltpu.roll(value, WIDE - 1, 1))

    def below(value):
        return pltpu.roll(value, 1, 0)

    def above(value):
        return pltpu.roll(value, ROWS - 1, 0)

    center, from_west, from_east, from_south, from_north = [coef_v[n] for n in range(5)]
    quantity = jnp.where(inside, state_v[0], 0.0)
    for t in range(SLOTS):
        quantity = (
            center * quantity + from_west * west(quantity) + from_east * east_of(quantity)
            + from_south * below(quantity) + from_north * above(quantity)
        )
        state_v[t] = quantity
    sens = jnp.zeros((ROWS, WIDE), F32)
    for t in reversed(range(SLOTS)):
        sens = sens + (dfull_v[t] * state_v[t] - bfull_v[t])
        sens = (
            center * sens + east_of(from_west * sens) + west(from_east * sens)
            + above(from_south * sens) + below(from_north * sens)
        )

    for c in range(3):
        ag_send[4 * c : 4 * c + 4, :] = sens[8:12, 128 * c : 128 * (c + 1)]

    def send_level(d, carry):
        pltpu.make_async_remote_copy(
            src_ref=ag_send, dst_ref=ag_recv.at[e],
            send_sem=send_sem.at[5], recv_sem=recv_sem.at[5],
            device_id={"ens": (e + d) % ENS}, device_id_type=MESH,
        ).start()
        return carry

    lax.fori_loop(1, ENS, send_level, 0)
    pltpu.make_async_copy(ag_send, ag_recv.at[e], recv_sem.at[5]).start()

    for h in range(2):
        pair = jnp.concatenate([state_v[2 * h, 8:12, :], state_v[2 * h + 1, 8:12, :]], axis=0)
        place = jnp.concatenate(wide_lon[2 * h : 2 * h + 2], axis=0)
        within = place & 127
        sampled = jnp.zeros((8, OBS), F32)
        for c in range(3):
            picked = jnp.take_along_axis(pair[:, 128 * c : 128 * (c + 1)], within, axis=1)
            sampled = jnp.where((place >> 7) == c, picked, sampled)
        dep_v[8 * h : 8 * h + 8, :] = sampled - jnp.concatenate(observed[2 * h : 2 * h + 2], axis=0)
    dep_copy = pltpu.make_async_copy(dep_v, dep_hbm, out_sem.at[0])
    dep_copy.start()

    pltpu.make_async_copy(ag_recv, ag_recv, recv_sem.at[5]).wait()
    products = []
    for i in range(TILE):
        level = jnp.concatenate([ag_recv[:, 4 * c + i, :] for c in range(3)], axis=1)
        products.append(
            (ensw_v[LEV * i : LEV * (i + 1), :] * level).astype(BF16).astype(F32)
        )
    products.append(jnp.zeros((128 - TILE * LEV, WIDE), F32))
    wide_v[...] = jnp.concatenate(products, axis=0).T
    by_lon = [wide_v[pl.ds(k, MP, stride=8), :] for k in range(KB)]
    for i in range(TILE):
        block = jnp.zeros((MP, 128), F32)
        for k in range(KB):
            block = jnp.where(group == k, pltpu.roll(by_lon[k], (16 * (k - i)) % 128, 1), block)
        rows_v[pl.ds(i, MP, stride=TILE), :] = block
    a2_send[...] = rows_v[...].reshape(MP, TILE, 128).astype(BF16)

    def send_product(d, carry):
        to = (q + d) % MP
        pltpu.make_async_remote_copy(
            src_ref=a2_send.at[to], dst_ref=a2_recv.at[q],
            send_sem=send_sem.at[6], recv_sem=recv_sem.at[6],
            device_id={"mp": to}, device_id_type=MESH,
        ).start()
        return carry

    lax.fori_loop(1, MP, send_product, 0)
    pltpu.make_async_copy(a2_send.at[q], a2_recv.at[q], recv_sem.at[6]).start()

    def sent(ref, n):
        pltpu.make_async_copy(ref, ref, send_sem.at[n]).wait()

    sent(a1_send.at[pl.ds(0, MP - 1)], 0)
    sent(wind_recv, 1)
    sent(db_recv, 2)
    sent(rs_recv, 3)
    sent(halo_recv, 4)
    sent(ag_recv.at[pl.ds(0, ENS - 1)], 5)
    dep_copy.wait()

    pltpu.make_async_copy(a2_recv, a2_recv, recv_sem.at[6]).wait()
    gathered = a2_recv[...].reshape(LAT, 128)
    smooth = lax.dot_general(
        gathered, kern_v[...], (((0,), (0,)), ((), ())), preferred_element_type=F32
    )
    grad_v[...] = smooth[0 : KB * LEV, :] + ctl_v[...].astype(F32)
    grad_copy = pltpu.make_async_copy(grad_v, grad_hbm, out_sem.at[1])
    grad_copy.start()
    sent(a2_send.at[pl.ds(0, MP - 1)], 6)
    grad_copy.wait()


def shards(
    ensemble, control, band, wind_east, wind_north, observation_longitude, innovation,
    observation_weight,
):
    operands = (
        ensemble.reshape(TILE * LEV, LON),
        jnp.transpose(control, (1, 3, 2, 0)).reshape(KB * LEV, LAT),
        band.reshape(1, LAT),
        wind_east.reshape(TILE * LEV, LON),
        wind_north.reshape(TILE * LEV, LON),
        observation_longitude,
        innovation.reshape(SLOTS * TILE * LEV, OBS),
        observation_weight,
    )
    anywhere = pl.BlockSpec(memory_space=pl.ANY)
    outs = (
        jax.ShapeDtypeStruct((KB * LEV, LAT), F32),
        jax.ShapeDtypeStruct((SLOTS * TILE, OBS), F32),
    )
    scratch = [pltpu.VMEM(x.shape, x.dtype) for x in operands]
    scratch += [pltpu.VMEM(x.shape, x.dtype) for x in outs]
    scratch += [
        pltpu.VMEM((LAT, LAT), BF16),
        pltpu.VMEM((LAT, 128), F32),
        pltpu.VMEM((WIDE, 128), F32),
        pltpu.VMEM((TILE * LEV, WIDE), F32),
        pltpu.VMEM((SLOTS, ROWS, WIDE), F32),
        pltpu.VMEM((MP, 8, 128), BF16),
        pltpu.VMEM((MP, 8, 128), BF16),
        pltpu.VMEM((LEV * 16, 128), F32),
        pltpu.VMEM((ENS - 1, 16, 128), F32),
        pltpu.VMEM((16, 128), F32),
        pltpu.VMEM((4, 16, 128), F32),
        pltpu.VMEM((8, WIDE), F32),
        pltpu.VMEM((4, 8, WIDE), F32),
        pltpu.VMEM((32, WIDE), F32),
        pltpu.VMEM((2, 32, WIDE), F32),
        pltpu.VMEM((5, ROWS, WIDE), F32),
        pltpu.VMEM((SLOTS, ROWS, WIDE), F32),
        pltpu.VMEM((SLOTS, ROWS, WIDE), F32),
        pltpu.VMEM((16, 128), F32),
        pltpu.VMEM((ENS, 16, 128), F32),
        pltpu.VMEM((MP, TILE, 128), BF16),
        pltpu.VMEM((MP, TILE, 128), BF16),
        pltpu.SemaphoreType.DMA((8,)),
        pltpu.SemaphoreType.DMA((2,)),
        pltpu.SemaphoreType.DMA((7,)),
        pltpu.SemaphoreType.DMA((7,)),
    ]
    gradient, departures = pl.pallas_call(
        body,
        out_shape=outs,
        in_specs=[anywhere] * len(operands),
        out_specs=(anywhere, anywhere),
        scratch_shapes=scratch,
        compiler_params=pltpu.CompilerParams(collective_id=0, has_side_effects=True),
        name="assimilate",
    )(*operands)
    gradient = jnp.transpose(gradient.reshape(1, KB, LEV, LAT), (3, 0, 2, 1))
    return gradient, departures.reshape(SLOTS, TILE, 1, OBS)


def solution(mesh):
    placed = (
        P("mp", "ens", None, None),
        P(None, "ens", None, "mp"),
        P(),
        P("mp", None, None),
        P("mp", None, None),
        P(None, "mp", None),
        P(None, "mp", None, None),
        P(None, "mp", None),
    )
    return jax.shard_map(
        shards,
        mesh=mesh,
        in_specs=placed,
        out_specs=(P(None, "ens", None, "mp"), P(None, "mp", "ens", None)),
        check_vma=False,
    )
```

```python
import jax
import jax.numpy as jnp
from jax import lax
from jax.experimental import pallas as pl
from jax.experimental.pallas import tpu as pltpu
from jax.sharding import PartitionSpec as P

MESH = pl.DeviceIdType.MESH
MP, ENS = 48, 16
LAT, LEV, LON, OBS, SLOTS = 192, 16, 288, 128, 4
TILE = 4
KB = 6
WIDE = MP * 8
LATP = 256
KROWS = 24
FIELDS = 80
F32, BF16 = jnp.float32, jnp.bfloat16


def iota(shape, dim):
    return lax.broadcasted_iota(jnp.int32, shape, dim)


def split3(value):
    first = value.astype(BF16)
    rest = value - first.astype(F32)
    second = rest.astype(BF16)
    third = (rest - second.astype(F32)).astype(BF16)
    return first.astype(F32), second.astype(F32), third.astype(F32)


def body(
    ens_hbm, ctl_hbm, band_hbm, east_hbm, north_hbm, lon_hbm, inn_hbm, wgt_hbm,
    grad_hbm, dep_hbm,
    ens_v, ctl_v, band_v, east_v, north_v, lon_v, inn_v, wgt_v, grad_v, dep_v,
    kern_v, rows_v, wide_v, spread_v, ensk_v, embed_v,
    a1_send, a1_recv, sparse_v, f_send, f_recv, fld_v, fld_near, fld_far,
    part_v, rs_recv, inc_v, halo_recv, state_v, coef_v, dfull_v, bfull_v,
    parts_v, s_send, s_recv, ag_send, ag_recv, samp_v,
    in_sem, out_sem, send_sem, recv_sem,
):
    q = lax.axis_index("mp")
    e = lax.axis_index("ens")

    barrier = pltpu.get_barrier_semaphore()

    def greet_mp(d, carry):
        pl.semaphore_signal(
            barrier, inc=1, device_id={"mp": (q + d) % MP}, device_id_type=MESH
        )
        return carry

    def greet_ens(d, carry):
        pl.semaphore_signal(
            barrier, inc=1, device_id={"ens": (e + d) % ENS}, device_id_type=MESH
        )
        return carry

    lax.fori_loop(1, MP, greet_mp, 0)
    lax.fori_loop(1, ENS, greet_ens, 0)
    pairs = [
        (ens_hbm, ens_v), (ctl_hbm, ctl_v), (band_hbm, band_v), (east_hbm, east_v),
        (north_hbm, north_v), (lon_hbm, lon_v), (inn_hbm, inn_v), (wgt_hbm, wgt_v),
    ]
    loads = [
        pltpu.make_async_copy(src, dst, in_sem.at[n]) for n, (src, dst) in enumerate(pairs)
    ]
    for copy in loads:
        copy.start()

    for ref in (sparse_v, fld_v, part_v, ag_send, state_v, dfull_v, bfull_v, parts_v):
        ref[...] = jnp.zeros_like(ref)

    source = iota((LON, WIDE), 1)
    embed_v[...] = (
        (iota((LON, WIDE), 0) == (source >> 3) * 6 + (source & 7)) & ((source & 7) < KB)
    ).astype(F32).astype(BF16)
    group = iota((MP, 128), 1) >> 4
    loads[0].wait()
    padded = jnp.dot(ens_v[...], embed_v[...], preferred_element_type=F32)
    wide_v[...] = jnp.concatenate([padded, jnp.zeros((128 - TILE * LEV, WIDE), F32)], axis=0).T
    by_lon = [wide_v[pl.ds(k, MP, stride=8), :] for k in range(KB)]
    for i in range(TILE):
        block = jnp.zeros((MP, 128), F32)
        for k in range(KB):
            block = jnp.where(group == k, pltpu.roll(by_lon[k], (16 * (k - i)) % 128, 1), block)
        rows_v[pl.ds(i, MP, stride=TILE), :] = block
    a1_send[...] = rows_v[...].reshape(MP, TILE, 128).astype(BF16)

    pl.semaphore_wait(barrier, MP + ENS - 2)

    def to_blocks(src, dst, n):
        def send(d, carry):
            to = (q + d) % MP
            pltpu.make_async_remote_copy(
                src_ref=src.at[to], dst_ref=dst.at[q],
                send_sem=send_sem.at[n], recv_sem=recv_sem.at[n],
                device_id={"mp": to}, device_id_type=MESH,
            ).start()
            return carry

        lax.fori_loop(1, MP, send, 0)
        pltpu.make_async_copy(src.at[q], dst.at[q], recv_sem.at[n]).start()

    def to_near(src, dst, slots, n):
        for slot, offset in slots:
            pltpu.make_async_remote_copy(
                src_ref=src, dst_ref=dst.at[slot], send_sem=send_sem.at[n],
                recv_sem=recv_sem.at[n],
                device_id={"mp": (q - offset + MP) % MP}, device_id_type=MESH,
            ).start()

    def arrived(ref, n):
        pltpu.make_async_copy(ref, ref, recv_sem.at[n]).wait()

    def sent(ref, n):
        pltpu.make_async_copy(ref, ref, send_sem.at[n]).wait()

    to_blocks(a1_send, a1_recv, 0)

    for copy in loads[3:]:
        copy.wait()
    mine = iota((LEV, LON), 0) == e
    winds = []
    for ref in (east_v, north_v):
        for i in range(TILE):
            level = ref[LEV * i : LEV * (i + 1), :].astype(F32)
            winds.append(jnp.sum(jnp.where(mine, level, 0.0), axis=0, keepdims=True))
    wide_winds = jnp.dot(
        jnp.concatenate(winds, axis=0).astype(BF16), embed_v[...], preferred_element_type=F32
    )
    for i in range(TILE):
        sparse_v[i, 64:65, :] = wide_winds[i : i + 1]
        sparse_v[i, 72:73, :] = wide_winds[TILE + i : TILE + i + 1]
    own_level = iota((LEV, OBS), 0) == e
    lane_rows = iota((WIDE, OBS), 0)
    blocks, inner, observed = [], [], []
    for t in range(SLOTS):
        lon = lon_v[t]
        block = (lon * 10923) >> 16
        place = lon + 2 * block
        blocks.append(block)
        inner.append(lon - 6 * block)
        weight = wgt_v[t]
        level_rows = []
        for i in range(TILE):
            start = LEV * (TILE * t + i)
            level_rows.append(
                jnp.sum(
                    jnp.where(own_level, inn_v[start : start + LEV, :], 0.0),
                    axis=0, keepdims=True,
                )
            )
        level_innovation = jnp.concatenate(level_rows, axis=0)
        observed.append(level_innovation)
        parts = split3(weight) + split3(weight * level_innovation)
        for i in range(TILE):
            hits = (lane_rows == place[i : i + 1, :]).astype(F32).astype(BF16)
            lhs = jnp.concatenate(
                [part[i : i + 1, :] for part in parts] + [jnp.zeros((2, OBS), F32)], axis=0
            ).astype(BF16)
            sums = lax.dot_general(
                lhs, hits, (((1,), (1,)), ((), ())), preferred_element_type=F32
            )
            sparse_v[i, 8 * t : 8 * t + 1, :] = sums[0:1] + sums[1:2] + sums[2:3]
            sparse_v[i, 32 + 8 * t : 33 + 8 * t, :] = sums[3:4] + sums[4:5] + sums[5:6]
    for i in range(TILE):
        wide_v[...] = sparse_v[i].T
        spaced = wide_v[pl.ds(0, MP, stride=8), :]
        for k in range(1, KB):
            spaced = spaced + pltpu.roll(wide_v[pl.ds(k, MP, stride=8), :], k, 1)
        rows_v[pl.ds(i, MP, stride=TILE), :] = spaced
    f_send[...] = rows_v[...].reshape(MP, TILE, 128)
    to_blocks(f_send, f_recv, 1)

    for copy in loads[1:3]:
        copy.wait()
    band = jnp.concatenate([band_v[...].astype(F32), jnp.ones((1, LATP - LAT), F32)], axis=1)
    width_j = jnp.broadcast_to(band, (LATP, LATP))
    width_i = width_j.T
    row, column = iota((LATP, LATP), 0), iota((LATP, LATP), 1)
    distance = jnp.abs(row - column).astype(F32)
    weights = jnp.maximum(0.0, 1.0 - 2.0 * distance / (width_i + width_j))
    kern_v[...] = jnp.where((row < LAT) & (column < LAT), weights, 0.0).astype(BF16)
    spread = jnp.dot(ctl_v[...], kern_v[0:LAT, :], preferred_element_type=F32)
    spread_v[...] = spread.astype(BF16).astype(F32)

    arrived(a1_recv, 0)
    gathered = a1_recv[...].astype(F32).reshape(LAT, 128)
    ensk = jnp.concatenate([gathered, jnp.zeros((LATP - LAT, 128), F32)], axis=0).T
    ensk_v[...] = ensk[0 : KB * LEV, :]
    part = ensk[0 : KB * LEV, :] * spread_v[...]
    for k in range(KB):
        for h in range(2):
            part_v[pl.ds(8 * h + k, LEV, stride=16), :] = part[
                LEV * k : LEV * (k + 1), 128 * h : 128 * (h + 1)
            ]

    def send_part(d, carry):
        to = (e + d) % ENS
        pltpu.make_async_remote_copy(
            src_ref=part_v.at[pl.ds(pl.multiple_of(to * 16, 16), 16)], dst_ref=rs_recv.at[d - 1],
            send_sem=send_sem.at[4], recv_sem=recv_sem.at[4],
            device_id={"ens": to}, device_id_type=MESH,
        ).start()
        return carry

    lax.fori_loop(1, ENS, send_part, 0)

    arrived(f_recv, 1)
    fields = f_recv[...].reshape(LAT, 128)
    fields = jnp.concatenate([fields, jnp.zeros((LATP - LAT, 128), F32)], axis=0).T
    fld_v[...] = fields[0:FIELDS, :]
    to_near(fld_v, fld_near, ((0, -1), (1, 1)), 2)
    to_near(fld_v.at[pl.ds(64, 16)], fld_far, ((0, -2), (1, 2)), 3)
    arrived(fld_near, 2)
    arrived(fld_far, 3)
    inside = (iota((KROWS, LATP), 1) < LAT) & (iota((KROWS, LATP), 0) < 22)
    blank = jnp.zeros((2, LATP), F32)
    winds = []
    for at in (0, 8):
        winds.append(
            jnp.concatenate(
                [
                    fld_far[0, at + 4 : at + 6, :], fld_near[0, 64 + at : 70 + at, :],
                    fld_v[64 + at : 70 + at, :], fld_near[1, 64 + at : 70 + at, :],
                    fld_far[1, at : at + 2, :], blank,
                ],
                axis=0,
            )
        )
    east, north = winds
    coefs = (
        1.0 - jnp.abs(east) - jnp.abs(north),
        jnp.maximum(east, 0.0), jnp.maximum(-east, 0.0),
        jnp.maximum(north, 0.0), jnp.maximum(-north, 0.0),
    )
    for n, coef in enumerate(coefs):
        coef_v[n] = jnp.where(inside, coef, 0.0)
    for t in range(SLOTS):
        for full, base in ((dfull_v, 8 * t), (bfull_v, 32 + 8 * t)):
            full[t, 2:8, :] = fld_near[0, base : base + 6, :]
            full[t, 8:14, :] = fld_v[base : base + 6, :]
            full[t, 14:20, :] = fld_near[1, base : base + 6, :]

    own_part = part_v[pl.ds(pl.multiple_of(e * 16, 16), 16), :]
    arrived(rs_recv, 4)
    total = own_part
    for d in range(ENS - 1):
        total = total + rs_recv[d]
    inc_v[:, 0:128] = total[0:8]
    inc_v[:, 128:256] = total[8:16]
    to_near(inc_v, halo_recv, ((0, -2), (1, -1), (2, 1), (3, 2)), 5)
    arrived(halo_recv, 5)
    state_v[0, 0:2, :] = halo_recv[0, 4:6, :]
    state_v[0, 2:8, :] = halo_recv[1, 0:6, :]
    state_v[0, 8:14, :] = inc_v[0:6, :]
    state_v[0, 14:20, :] = halo_recv[2, 0:6, :]
    state_v[0, 20:22, :] = halo_recv[3, 0:2, :]

    def west(value):
        return pltpu.roll(value, 1, 0)

    def east_of(value):
        return pltpu.roll(value, KROWS - 1, 0)

    def below(value):
        return pltpu.roll(value, 1, 1)

    def above(value):
        return pltpu.roll(value, LATP - 1, 1)

    center, from_west, from_east, from_south, from_north = [coef_v[n] for n in range(5)]
    quantity = state_v[0]
    for t in range(SLOTS):
        quantity = (
            center * quantity + from_west * west(quantity) + from_east * east_of(quantity)
            + from_south * below(quantity) + from_north * above(quantity)
        )
        state_v[t] = quantity
        for n, piece in enumerate(split3(quantity[8:14, :])):
            parts_v[32 * n + 8 * t : 32 * n + 8 * t + 6, :] = piece

    s_send[...] = parts_v[...].T[0:LAT, :].reshape(MP, TILE, 128).astype(BF16)
    to_blocks(s_send, s_recv, 6)

    sens = jnp.zeros((KROWS, LATP), F32)
    for t in reversed(range(SLOTS)):
        sens = sens + (dfull_v[t] * state_v[t] - bfull_v[t])
        sens = (
            center * sens + east_of(from_west * sens) + west(from_east * sens)
            + above(from_south * sens) + below(from_north * sens)
        )
    ag_send[0:KB, :] = sens[8:14, :]

    def send_level(d, carry):
        pltpu.make_async_remote_copy(
            src_ref=ag_send, dst_ref=ag_recv.at[e],
            send_sem=send_sem.at[7], recv_sem=recv_sem.at[7],
            device_id={"ens": (e + d) % ENS}, device_id_type=MESH,
        ).start()
        return carry

    lax.fori_loop(1, ENS, send_level, 0)
    pltpu.make_async_copy(ag_send, ag_recv.at[e], recv_sem.at[7]).start()

    sent(a1_send.at[pl.ds(0, MP - 1)], 0)
    sent(f_send.at[pl.ds(0, MP - 1)], 1)
    sent(fld_near, 2)
    sent(fld_far, 3)
    sent(rs_recv, 4)
    sent(halo_recv, 5)

    arrived(ag_recv, 7)
    products = jnp.concatenate(
        [
            (ensk_v[LEV * k : LEV * (k + 1), :] * ag_recv[:, k, :]).astype(BF16).astype(F32)
            for k in range(KB)
        ],
        axis=0,
    ).astype(BF16)
    smooth = jnp.dot(products, kern_v[...], preferred_element_type=F32)
    grad_v[...] = smooth[:, 0:LAT] + ctl_v[...].astype(F32)
    grad_copy = pltpu.make_async_copy(grad_v, grad_hbm, out_sem.at[1])
    grad_copy.start()

    arrived(s_recv, 6)
    states = s_recv[...].astype(F32).reshape(LAT, 128)
    states = jnp.concatenate([states, jnp.zeros((LATP - LAT, 128), F32)], axis=0).T
    samp_v[...] = states[0:32, :] + states[32:64, :] + states[64:96, :]
    tile_row = iota((8, OBS), 0) & 3
    for h in range(2):
        block = jnp.concatenate(blocks[2 * h : 2 * h + 2], axis=0)
        lon_in = jnp.concatenate(inner[2 * h : 2 * h + 2], axis=0)
        index = TILE * block + tile_row
        within, half = index & 127, index >> 7
        sampled = jnp.zeros((8, OBS), F32)
        for k in range(KB):
            at = 16 * h + k
            both = jnp.concatenate(
                [
                    jnp.broadcast_to(samp_v[at : at + 1, :], (TILE, LATP)),
                    jnp.broadcast_to(samp_v[at + 8 : at + 9, :], (TILE, LATP)),
                ],
                axis=0,
            )
            low = jnp.take_along_axis(both[:, 0:128], within, axis=1)
            high = jnp.take_along_axis(both[:, 128:256], within, axis=1)
            sampled = jnp.where(lon_in == k, jnp.where(half == 0, low, high), sampled)
        dep_v[8 * h : 8 * h + 8, :] = sampled - jnp.concatenate(observed[2 * h : 2 * h + 2], axis=0)
    dep_copy = pltpu.make_async_copy(dep_v, dep_hbm, out_sem.at[0])
    dep_copy.start()
    sent(s_send.at[pl.ds(0, MP - 1)], 6)
    sent(ag_recv.at[pl.ds(0, ENS - 1)], 7)
    dep_copy.wait()
    grad_copy.wait()


def shards(
    ensemble, control, band, wind_east, wind_north, observation_longitude, innovation,
    observation_weight,
):
    operands = (
        ensemble.reshape(TILE * LEV, LON),
        jnp.transpose(control, (1, 3, 2, 0)).reshape(KB * LEV, LAT),
        band.reshape(1, LAT),
        wind_east.reshape(TILE * LEV, LON),
        wind_north.reshape(TILE * LEV, LON),
        observation_longitude,
        innovation.reshape(SLOTS * TILE * LEV, OBS),
        observation_weight,
    )
    operands = tuple(pltpu.with_memory_space_constraint(x, pltpu.HBM) for x in operands)
    anywhere = pl.BlockSpec(memory_space=pl.ANY)
    outs = (
        jax.ShapeDtypeStruct((KB * LEV, LAT), F32),
        jax.ShapeDtypeStruct((SLOTS * TILE, OBS), F32),
    )
    scratch = [pltpu.VMEM(x.shape, x.dtype) for x in operands]
    scratch += [pltpu.VMEM(x.shape, x.dtype) for x in outs]
    scratch += [
        pltpu.VMEM((LATP, LATP), BF16),
        pltpu.VMEM((LAT, 128), F32),
        pltpu.VMEM((WIDE, 128), F32),
        pltpu.VMEM((KB * LEV, LATP), F32),
        pltpu.VMEM((KB * LEV, LATP), F32),
        pltpu.VMEM((LON, WIDE), BF16),
        pltpu.VMEM((MP, TILE, 128), BF16),
        pltpu.VMEM((MP, TILE, 128), BF16),
        pltpu.VMEM((TILE, 128, WIDE), F32),
        pltpu.VMEM((MP, TILE, 128), F32),
        pltpu.VMEM((MP, TILE, 128), F32),
        pltpu.VMEM((FIELDS, LATP), F32),
        pltpu.VMEM((2, FIELDS, LATP), F32),
        pltpu.VMEM((2, 16, LATP), F32),
        pltpu.VMEM((LEV * 16, 128), F32),
        pltpu.VMEM((ENS - 1, 16, 128), F32),
        pltpu.VMEM((8, LATP), F32),
        pltpu.VMEM((4, 8, LATP), F32),
        pltpu.VMEM((SLOTS, KROWS, LATP), F32),
        pltpu.VMEM((5, KROWS, LATP), F32),
        pltpu.VMEM((SLOTS, KROWS, LATP), F32),
        pltpu.VMEM((SLOTS, KROWS, LATP), F32),
        pltpu.VMEM((128, LATP), F32),
        pltpu.VMEM((MP, TILE, 128), BF16),
        pltpu.VMEM((MP, TILE, 128), BF16),
        pltpu.VMEM((8, LATP), F32),
        pltpu.VMEM((ENS, 8, LATP), F32),
        pltpu.VMEM((32, LATP), F32),
        pltpu.SemaphoreType.DMA((8,)),
        pltpu.SemaphoreType.DMA((2,)),
        pltpu.SemaphoreType.DMA((8,)),
        pltpu.SemaphoreType.DMA((8,)),
    ]
    gradient, departures = pl.pallas_call(
        body,
        out_shape=outs,
        in_specs=[anywhere] * len(operands),
        out_specs=(anywhere, anywhere),
        scratch_shapes=scratch,
        compiler_params=pltpu.CompilerParams(
            collective_id=0, has_side_effects=True, vmem_limit_bytes=16 * 1024 * 1024
        ),
        name="assimilate",
    )(*operands)
    gradient = jnp.transpose(gradient.reshape(1, KB, LEV, LAT), (3, 0, 2, 1))
    return gradient, departures.reshape(SLOTS, TILE, 1, OBS)


def solution(mesh):
    placed = (
        P("mp", "ens", None, None),
        P(None, "ens", None, "mp"),
        P(),
        P("mp", None, None),
        P("mp", None, None),
        P(None, "mp", None),
        P(None, "mp", None, None),
        P(None, "mp", None),
    )
    return jax.shard_map(
        shards,
        mesh=mesh,
        in_specs=placed,
        out_specs=(P(None, "ens", None, "mp"), P(None, "mp", "ens", None)),
        check_vma=False,
    )
```

```python
import jax
import jax.numpy as jnp
from jax import lax
from jax.experimental import pallas as pl
from jax.experimental.pallas import tpu as pltpu
from jax.sharding import PartitionSpec as P

MESH = pl.DeviceIdType.MESH
MP, ENS = 48, 16
PLANES, PLANE = 3, 16
LAT, LEV, LON, OBS, SLOTS = 192, 16, 288, 128, 4
FARTHEST = sorted(
    [(z, y, c) for z in range(PLANES) for y in range(8) for c in range(2) if z or y or c],
    key=lambda d: (-4 * (d[0] > 0) - min(d[1], 8 - d[1]), d),
)
TILE = 4
KB = 6
WIDE = MP * 8
LATP = 256
KROWS = 24
FIELDS = 80
F32, BF16 = jnp.float32, jnp.bfloat16


def iota(shape, dim):
    return lax.broadcasted_iota(jnp.int32, shape, dim)


def split3(value):
    first = value.astype(BF16)
    rest = value - first.astype(F32)
    second = rest.astype(BF16)
    third = (rest - second.astype(F32)).astype(BF16)
    return first.astype(F32), second.astype(F32), third.astype(F32)


def body(
    ens_hbm, ctl_hbm, band_hbm, east_hbm, north_hbm, lon_hbm, inn_hbm, wgt_hbm,
    grad_v, dep_v,
    ens_v, ctl_v, band_v, east_v, north_v, lon_v, inn_v, wgt_v,
    kern_v, rows_v, wide_v, spread_v, ensk_v, embed_v,
    a1_send, a1_mid, a1_recv, sparse_v, f_send, f_mid, f_recv, fld_v, fld_near, fld_far,
    part_v, rs_recv, inc_v, halo_recv, state_v, coef_v, dfull_v, bfull_v,
    parts_v, s_send, s_recv, ag_send, ag_recv, samp_v,
    in_sem, send_sem, recv_sem,
):
    q = lax.axis_index("mp")
    e = lax.axis_index("ens")
    plane, rank = q // PLANE, q % PLANE

    barrier = pltpu.get_barrier_semaphore()

    def greet_plane(d, carry):
        pl.semaphore_signal(
            barrier, inc=1, device_id={"mp": plane * PLANE + (rank + d) % PLANE},
            device_id_type=MESH,
        )
        return carry

    def greet_line(d, carry):
        pl.semaphore_signal(
            barrier, inc=1, device_id={"mp": (q + PLANE * d) % MP}, device_id_type=MESH
        )
        return carry

    def greet_ens(d, carry):
        pl.semaphore_signal(
            barrier, inc=1, device_id={"ens": (e + d) % ENS}, device_id_type=MESH
        )
        return carry

    lax.fori_loop(1, ENS, greet_ens, 0)
    lax.fori_loop(1, PLANES, greet_line, 0)
    lax.fori_loop(1, PLANE, greet_plane, 0)
    pairs = [
        (ens_hbm, ens_v), (ctl_hbm, ctl_v), (band_hbm, band_v), (east_hbm, east_v),
        (north_hbm, north_v), (lon_hbm, lon_v), (inn_hbm, inn_v), (wgt_hbm, wgt_v),
    ]
    loads = [
        pltpu.make_async_copy(src, dst, in_sem.at[n]) for n, (src, dst) in enumerate(pairs)
    ]
    for copy in loads:
        copy.start()

    for ref in (sparse_v, fld_v, part_v, ag_send, state_v, dfull_v, bfull_v, parts_v):
        ref[...] = jnp.zeros_like(ref)

    source = iota((LON, WIDE), 1)
    embed_v[...] = (
        (iota((LON, WIDE), 0) == (source >> 3) * 6 + (source & 7)) & ((source & 7) < KB)
    ).astype(F32).astype(BF16)
    group = iota((MP, 128), 1) >> 4
    loads[0].wait()
    padded = jnp.dot(ens_v[...], embed_v[...], preferred_element_type=F32)
    wide_v[...] = jnp.concatenate([padded, jnp.zeros((128 - TILE * LEV, WIDE), F32)], axis=0).T
    by_lon = [wide_v[pl.ds(k, MP, stride=8), :] for k in range(KB)]
    for i in range(TILE):
        block = jnp.zeros((MP, 128), F32)
        for k in range(KB):
            block = jnp.where(group == k, pltpu.roll(by_lon[k], (16 * (k - i)) % 128, 1), block)
        rows_v[pl.ds(i, MP, stride=TILE), :] = block
    a1_send[...] = rows_v[...].reshape(PLANES, PLANE, TILE, 128).astype(BF16)

    pl.semaphore_wait(barrier, PLANE + PLANES + ENS - 3)

    def to_plane(src, middle, n):
        def send(d, carry):
            to = (rank + d) % PLANE
            pltpu.make_async_remote_copy(
                src_ref=src.at[:, to], dst_ref=middle.at[rank],
                send_sem=send_sem.at[n], recv_sem=recv_sem.at[n],
                device_id={"mp": plane * PLANE + to}, device_id_type=MESH,
            ).start()
            return carry

        lax.fori_loop(1, PLANE, send, 0)
        pltpu.make_async_copy(src.at[:, rank], middle.at[rank], recv_sem.at[n]).start()

    def to_line(middle, dst, n):
        for d in range(1, PLANES):
            to = (plane + d) % PLANES
            pltpu.make_async_remote_copy(
                src_ref=middle.at[:, to], dst_ref=dst.at[plane],
                send_sem=send_sem.at[n], recv_sem=recv_sem.at[n],
                device_id={"mp": to * PLANE + rank}, device_id_type=MESH,
            ).start()
        pltpu.make_async_copy(middle.at[:, plane], dst.at[plane], recv_sem.at[n]).start()

    def to_all(src, dst, n):
        for dz, dy, dc in FARTHEST:
            to_z = (plane + dz) % PLANES
            to_r = (rank // 2 + dy) % 8 * 2 + (rank + dc) % 2
            pltpu.make_async_remote_copy(
                src_ref=src.at[to_z, to_r], dst_ref=dst.at[plane, rank],
                send_sem=send_sem.at[n], recv_sem=recv_sem.at[n],
                device_id={"mp": to_z * PLANE + to_r}, device_id_type=MESH,
            ).start()
        pltpu.make_async_copy(src.at[plane, rank], dst.at[plane, rank], recv_sem.at[n]).start()

    def to_near(src, dst, slots, n):
        for slot, offset in slots:
            pltpu.make_async_remote_copy(
                src_ref=src, dst_ref=dst.at[slot], send_sem=send_sem.at[n],
                recv_sem=recv_sem.at[n],
                device_id={"mp": (q - offset + MP) % MP}, device_id_type=MESH,
            ).start()

    def arrived(ref, n):
        pltpu.make_async_copy(ref, ref, recv_sem.at[n]).wait()

    def sent(ref, n):
        pltpu.make_async_copy(ref, ref, send_sem.at[n]).wait()

    to_plane(a1_send, a1_mid, 0)

    for copy in loads[3:]:
        copy.wait()
    mine = iota((LEV, LON), 0) == e
    winds = []
    for ref in (east_v, north_v):
        for i in range(TILE):
            level = ref[LEV * i : LEV * (i + 1), :].astype(F32)
            winds.append(jnp.sum(jnp.where(mine, level, 0.0), axis=0, keepdims=True))
    wide_winds = jnp.dot(
        jnp.concatenate(winds, axis=0).astype(BF16), embed_v[...], preferred_element_type=F32
    )
    for i in range(TILE):
        sparse_v[i, 64:65, :] = wide_winds[i : i + 1]
        sparse_v[i, 72:73, :] = wide_winds[TILE + i : TILE + i + 1]
    own_level = iota((LEV, OBS), 0) == e
    lane_rows = iota((WIDE, OBS), 0)
    blocks, inner, observed = [], [], []
    for t in range(SLOTS):
        lon = lon_v[t]
        block = (lon * 10923) >> 16
        place = lon + 2 * block
        blocks.append(block)
        inner.append(lon - 6 * block)
        weight = wgt_v[t]
        level_rows = []
        for i in range(TILE):
            start = LEV * (TILE * t + i)
            level_rows.append(
                jnp.sum(
                    jnp.where(own_level, inn_v[start : start + LEV, :], 0.0),
                    axis=0, keepdims=True,
                )
            )
        level_innovation = jnp.concatenate(level_rows, axis=0)
        observed.append(level_innovation)
        parts = split3(weight) + split3(weight * level_innovation)
        for i in range(TILE):
            hits = (lane_rows == place[i : i + 1, :]).astype(F32).astype(BF16)
            lhs = jnp.concatenate(
                [part[i : i + 1, :] for part in parts] + [jnp.zeros((2, OBS), F32)], axis=0
            ).astype(BF16)
            sums = lax.dot_general(
                lhs, hits, (((1,), (1,)), ((), ())), preferred_element_type=F32
            )
            sparse_v[i, 8 * t : 8 * t + 1, :] = sums[0:1] + sums[1:2] + sums[2:3]
            sparse_v[i, 32 + 8 * t : 33 + 8 * t, :] = sums[3:4] + sums[4:5] + sums[5:6]
    for i in range(TILE):
        wide_v[...] = sparse_v[i].T
        spaced = wide_v[pl.ds(0, MP, stride=8), :]
        for k in range(1, KB):
            spaced = spaced + pltpu.roll(wide_v[pl.ds(k, MP, stride=8), :], k, 1)
        rows_v[pl.ds(i, MP, stride=TILE), :] = spaced
    f_send[...] = rows_v[...].reshape(PLANES, PLANE, TILE, 128)
    to_plane(f_send, f_mid, 1)
    arrived(a1_mid, 0)
    to_line(a1_mid, a1_recv, 8)

    for copy in loads[1:3]:
        copy.wait()
    band = jnp.concatenate([band_v[...].astype(F32), jnp.ones((1, LATP - LAT), F32)], axis=1)
    width_j = jnp.broadcast_to(band, (LATP, LATP))
    width_i = width_j.T
    row, column = iota((LATP, LATP), 0), iota((LATP, LATP), 1)
    distance = jnp.abs(row - column).astype(F32)
    weights = jnp.maximum(0.0, 1.0 - 2.0 * distance / (width_i + width_j))
    kern_v[...] = jnp.where((row < LAT) & (column < LAT), weights, 0.0).astype(BF16)
    spread = jnp.dot(ctl_v[...], kern_v[0:LAT, :], preferred_element_type=F32)
    spread_v[...] = spread.astype(BF16).astype(F32)

    arrived(f_mid, 1)
    to_line(f_mid, f_recv, 9)
    arrived(a1_recv, 8)
    gathered = a1_recv[...].astype(F32).reshape(LAT, 128)
    ensk = jnp.concatenate([gathered, jnp.zeros((LATP - LAT, 128), F32)], axis=0).T
    ensk_v[...] = ensk[0 : KB * LEV, :]
    part = ensk[0 : KB * LEV, :] * spread_v[...]
    for k in range(KB):
        for h in range(2):
            part_v[pl.ds(8 * h + k, LEV, stride=16), :] = part[
                LEV * k : LEV * (k + 1), 128 * h : 128 * (h + 1)
            ]

    def send_part(d, carry):
        to = (e + d) % ENS
        pltpu.make_async_remote_copy(
            src_ref=part_v.at[pl.ds(pl.multiple_of(to * 16, 16), 16)], dst_ref=rs_recv.at[d - 1],
            send_sem=send_sem.at[4], recv_sem=recv_sem.at[4],
            device_id={"ens": to}, device_id_type=MESH,
        ).start()
        return carry

    lax.fori_loop(1, ENS, send_part, 0)

    arrived(f_recv, 9)
    fields = f_recv[...].reshape(LAT, 128)
    fields = jnp.concatenate([fields, jnp.zeros((LATP - LAT, 128), F32)], axis=0).T
    fld_v[...] = fields[0:FIELDS, :]
    to_near(fld_v, fld_near, ((0, -1), (1, 1)), 2)
    to_near(fld_v.at[pl.ds(64, 16)], fld_far, ((0, -2), (1, 2)), 3)
    own_part = part_v[pl.ds(pl.multiple_of(e * 16, 16), 16), :]
    arrived(rs_recv, 4)
    total = own_part
    for d in range(ENS - 1):
        total = total + rs_recv[d]
    inc_v[:, 0:128] = total[0:8]
    inc_v[:, 128:256] = total[8:16]
    to_near(inc_v, halo_recv, ((0, -2), (1, -1), (2, 1), (3, 2)), 5)
    arrived(fld_near, 2)
    arrived(fld_far, 3)
    inside = (iota((KROWS, LATP), 1) < LAT) & (iota((KROWS, LATP), 0) < 22)
    blank = jnp.zeros((2, LATP), F32)
    winds = []
    for at in (0, 8):
        winds.append(
            jnp.concatenate(
                [
                    fld_far[0, at + 4 : at + 6, :], fld_near[0, 64 + at : 70 + at, :],
                    fld_v[64 + at : 70 + at, :], fld_near[1, 64 + at : 70 + at, :],
                    fld_far[1, at : at + 2, :], blank,
                ],
                axis=0,
            )
        )
    east, north = winds
    coefs = (
        1.0 - jnp.abs(east) - jnp.abs(north),
        jnp.maximum(east, 0.0), jnp.maximum(-east, 0.0),
        jnp.maximum(north, 0.0), jnp.maximum(-north, 0.0),
    )
    for n, coef in enumerate(coefs):
        coef_v[n] = jnp.where(inside, coef, 0.0)
    for t in range(SLOTS):
        for full, base in ((dfull_v, 8 * t), (bfull_v, 32 + 8 * t)):
            full[t, 2:8, :] = fld_near[0, base : base + 6, :]
            full[t, 8:14, :] = fld_v[base : base + 6, :]
            full[t, 14:20, :] = fld_near[1, base : base + 6, :]

    arrived(halo_recv, 5)
    state_v[0, 0:2, :] = halo_recv[0, 4:6, :]
    state_v[0, 2:8, :] = halo_recv[1, 0:6, :]
    state_v[0, 8:14, :] = inc_v[0:6, :]
    state_v[0, 14:20, :] = halo_recv[2, 0:6, :]
    state_v[0, 20:22, :] = halo_recv[3, 0:2, :]

    def west(value):
        return pltpu.roll(value, 1, 0)

    def east_of(value):
        return pltpu.roll(value, KROWS - 1, 0)

    def below(value):
        return pltpu.roll(value, 1, 1)

    def above(value):
        return pltpu.roll(value, LATP - 1, 1)

    center, from_west, from_east, from_south, from_north = [coef_v[n] for n in range(5)]
    quantity = state_v[0]
    for t in range(SLOTS):
        quantity = (
            center * quantity + from_west * west(quantity) + from_east * east_of(quantity)
            + from_south * below(quantity) + from_north * above(quantity)
        )
        state_v[t] = quantity
        for n, piece in enumerate(split3(quantity[8:14, :])):
            parts_v[32 * n + 8 * t : 32 * n + 8 * t + 6, :] = piece

    s_send[...] = parts_v[...].T[0:LAT, :].reshape(PLANES, PLANE, TILE, 128).astype(BF16)
    to_all(s_send, s_recv, 6)

    sens = jnp.zeros((KROWS, LATP), F32)
    for t in reversed(range(SLOTS)):
        sens = sens + (dfull_v[t] * state_v[t] - bfull_v[t])
        sens = (
            center * sens + east_of(from_west * sens) + west(from_east * sens)
            + above(from_south * sens) + below(from_north * sens)
        )
    ag_send[0:KB, :] = sens[8:14, :]

    def send_level(d, carry):
        pltpu.make_async_remote_copy(
            src_ref=ag_send, dst_ref=ag_recv.at[e],
            send_sem=send_sem.at[7], recv_sem=recv_sem.at[7],
            device_id={"ens": (e + d) % ENS}, device_id_type=MESH,
        ).start()
        return carry

    lax.fori_loop(1, ENS, send_level, 0)
    pltpu.make_async_copy(ag_send, ag_recv.at[e], recv_sem.at[7]).start()

    sent(a1_mid.at[pl.ds(0, PLANE - 1)], 0)
    sent(a1_recv.at[pl.ds(0, PLANES - 1)], 8)
    sent(f_mid.at[pl.ds(0, PLANE - 1)], 1)
    sent(f_recv.at[pl.ds(0, PLANES - 1)], 9)
    sent(fld_near, 2)
    sent(fld_far, 3)
    sent(rs_recv, 4)
    sent(halo_recv, 5)

    arrived(ag_recv, 7)
    products = jnp.concatenate(
        [
            (ensk_v[LEV * k : LEV * (k + 1), :] * ag_recv[:, k, :]).astype(BF16).astype(F32)
            for k in range(KB)
        ],
        axis=0,
    ).astype(BF16)
    smooth = jnp.dot(products, kern_v[...], preferred_element_type=F32)
    grad_v[...] = smooth[:, 0:LAT] + ctl_v[...].astype(F32)

    arrived(s_recv, 6)
    states = s_recv[...].astype(F32).reshape(LAT, 128)
    states = jnp.concatenate([states, jnp.zeros((LATP - LAT, 128), F32)], axis=0).T
    samp_v[...] = states[0:32, :] + states[32:64, :] + states[64:96, :]
    tile_row = iota((8, OBS), 0) & 3
    for h in range(2):
        block = jnp.concatenate(blocks[2 * h : 2 * h + 2], axis=0)
        lon_in = jnp.concatenate(inner[2 * h : 2 * h + 2], axis=0)
        index = TILE * block + tile_row
        within, half = index & 127, index >> 7
        sampled = jnp.zeros((8, OBS), F32)
        for k in range(KB):
            at = 16 * h + k
            both = jnp.concatenate(
                [
                    jnp.broadcast_to(samp_v[at : at + 1, :], (TILE, LATP)),
                    jnp.broadcast_to(samp_v[at + 8 : at + 9, :], (TILE, LATP)),
                ],
                axis=0,
            )
            low = jnp.take_along_axis(both[:, 0:128], within, axis=1)
            high = jnp.take_along_axis(both[:, 128:256], within, axis=1)
            sampled = jnp.where(lon_in == k, jnp.where(half == 0, low, high), sampled)
        dep_v[8 * h : 8 * h + 8, :] = sampled - jnp.concatenate(observed[2 * h : 2 * h + 2], axis=0)
    sent(s_recv.at[0], 6)
    sent(s_recv.at[1], 6)
    sent(s_recv.at[2, pl.ds(0, PLANE - 1)], 6)
    sent(ag_recv.at[pl.ds(0, ENS - 1)], 7)


def move_out(grad_v, dep_v, grad_hbm, dep_hbm, out_sem):
    copies = [
        pltpu.make_async_copy(grad_v, grad_hbm, out_sem.at[0]),
        pltpu.make_async_copy(dep_v, dep_hbm, out_sem.at[1]),
    ]
    for copy in copies:
        copy.start()
    for copy in copies:
        copy.wait()


def shards(
    ensemble, control, band, wind_east, wind_north, observation_longitude, innovation,
    observation_weight,
):
    operands = (
        ensemble.reshape(TILE * LEV, LON),
        jnp.transpose(control, (1, 3, 2, 0)).reshape(KB * LEV, LAT),
        band.reshape(1, LAT),
        wind_east.reshape(TILE * LEV, LON),
        wind_north.reshape(TILE * LEV, LON),
        observation_longitude,
        innovation.reshape(SLOTS * TILE * LEV, OBS),
        observation_weight,
    )
    operands = tuple(pltpu.with_memory_space_constraint(x, pltpu.HBM) for x in operands)
    anywhere = pl.BlockSpec(memory_space=pl.ANY)
    outs = (
        jax.ShapeDtypeStruct((KB * LEV, LAT), F32),
        jax.ShapeDtypeStruct((SLOTS * TILE, OBS), F32),
    )
    scratch = [pltpu.VMEM(x.shape, x.dtype) for x in operands]
    scratch += [
        pltpu.VMEM((LATP, LATP), BF16),
        pltpu.VMEM((LAT, 128), F32),
        pltpu.VMEM((WIDE, 128), F32),
        pltpu.VMEM((KB * LEV, LATP), F32),
        pltpu.VMEM((KB * LEV, LATP), F32),
        pltpu.VMEM((LON, WIDE), BF16),
        pltpu.VMEM((PLANES, PLANE, TILE, 128), BF16),
        pltpu.VMEM((PLANE, PLANES, TILE, 128), BF16),
        pltpu.VMEM((PLANES, PLANE, TILE, 128), BF16),
        pltpu.VMEM((TILE, 128, WIDE), F32),
        pltpu.VMEM((PLANES, PLANE, TILE, 128), F32),
        pltpu.VMEM((PLANE, PLANES, TILE, 128), F32),
        pltpu.VMEM((PLANES, PLANE, TILE, 128), F32),
        pltpu.VMEM((FIELDS, LATP), F32),
        pltpu.VMEM((2, FIELDS, LATP), F32),
        pltpu.VMEM((2, 16, LATP), F32),
        pltpu.VMEM((LEV * 16, 128), F32),
        pltpu.VMEM((ENS - 1, 16, 128), F32),
        pltpu.VMEM((8, LATP), F32),
        pltpu.VMEM((4, 8, LATP), F32),
        pltpu.VMEM((SLOTS, KROWS, LATP), F32),
        pltpu.VMEM((5, KROWS, LATP), F32),
        pltpu.VMEM((SLOTS, KROWS, LATP), F32),
        pltpu.VMEM((SLOTS, KROWS, LATP), F32),
        pltpu.VMEM((128, LATP), F32),
        pltpu.VMEM((PLANES, PLANE, TILE, 128), BF16),
        pltpu.VMEM((PLANES, PLANE, TILE, 128), BF16),
        pltpu.VMEM((8, LATP), F32),
        pltpu.VMEM((ENS, 8, LATP), F32),
        pltpu.VMEM((32, LATP), F32),
        pltpu.SemaphoreType.DMA((8,)),
        pltpu.SemaphoreType.DMA((10,)),
        pltpu.SemaphoreType.DMA((10,)),
    ]
    gradient, departures = pl.pallas_call(
        body,
        out_shape=outs,
        in_specs=[anywhere] * len(operands),
        out_specs=(pl.BlockSpec(memory_space=pltpu.VMEM),) * 2,
        scratch_shapes=scratch,
        compiler_params=pltpu.CompilerParams(
            collective_id=0, has_side_effects=True, vmem_limit_bytes=16 * 1024 * 1024
        ),
        name="assimilate",
    )(*operands)
    gradient, departures = pl.pallas_call(
        move_out,
        out_shape=outs,
        in_specs=[anywhere] * 2,
        out_specs=(pl.BlockSpec(memory_space=pltpu.HBM),) * 2,
        scratch_shapes=[pltpu.SemaphoreType.DMA((2,))],
        compiler_params=pltpu.CompilerParams(vmem_limit_bytes=1024 * 1024),
        name="move_out",
    )(gradient, departures)
    gradient = jnp.transpose(gradient.reshape(1, KB, LEV, LAT), (3, 0, 2, 1))
    return gradient, departures.reshape(SLOTS, TILE, 1, OBS)


def solution(mesh):
    placed = (
        P("mp", "ens", None, None),
        P(None, "ens", None, "mp"),
        P(),
        P("mp", None, None),
        P("mp", None, None),
        P(None, "mp", None),
        P(None, "mp", None, None),
        P(None, "mp", None),
    )
    return jax.shard_map(
        shards,
        mesh=mesh,
        in_specs=placed,
        out_specs=(P(None, "ens", None, "mp"), P(None, "mp", "ens", None)),
        check_vma=False,
    )
```

```python
import jax
import jax.numpy as jnp
from jax import lax
from jax.experimental import pallas as pl
from jax.experimental.pallas import tpu as pltpu
from jax.sharding import PartitionSpec as P

MESH = pl.DeviceIdType.MESH
MP, ENS = 48, 16
PLANES, PLANE = 3, 16
LAT, LEV, LON, OBS, SLOTS = 192, 16, 288, 128, 4
LEVEL_ORDER = (8, 9, 7, 10, 6, 11, 5, 12, 4, 13, 3, 14, 2, 15, 1)
TILE = 4
KB = 6
WIDE = MP * 8
LATP = 256
KROWS = 24
TROWS = 16
PART, PART2 = jnp.bfloat16, jnp.bfloat16
SENS = jnp.bfloat16
FIELDS = 64
F32, BF16 = jnp.float32, jnp.bfloat16


def iota(shape, dim):
    return lax.broadcasted_iota(jnp.int32, shape, dim)


def split3(value):
    first = value.astype(BF16)
    rest = value - first.astype(F32)
    second = rest.astype(BF16)
    third = (rest - second.astype(F32)).astype(BF16)
    return first.astype(F32), second.astype(F32), third.astype(F32)


def body(
    ens_hbm, ctl_hbm, band_hbm, east_hbm, north_hbm, lon_hbm, inn_hbm, wgt_hbm,
    grad_v, dep_v,
    ens_v, ctl_v, band_v, east_v, north_v, lon_v, inn_v, wgt_v,
    kern_v, rows_v, wide_v, spread_v, ensk_v, embed_v,
    a1_send, a1_mid, a1_recv, sparse_v, f_send, f_mid, f_recv, fld_v, fldn_s, fld_near, fldw_v, fldw_s, fldw_recv, pairs_v,
    part_v, part_s, rs_recv, inc_v, halo_recv, state_v, coef_v, dfull_v, bfull_v,
    ag_send, ag_recv, level_v,
    ensw_v, b_send, b_mid, b_recv, part2_v, part2_s, rs2_recv, inc2_v, halo2_recv,
    wind_v, wind_recv, state2_v, coef2_v,
    in_sem, send_sem, recv_sem,
):
    q = lax.axis_index("mp")
    e = lax.axis_index("ens")
    plane, rank = q // PLANE, q % PLANE

    barrier = pltpu.get_barrier_semaphore()

    def greet_plane(d, carry):
        pl.semaphore_signal(
            barrier, inc=1, device_id={"mp": plane * PLANE + (rank + d) % PLANE},
            device_id_type=MESH,
        )
        return carry

    def greet_line(d, carry):
        pl.semaphore_signal(
            barrier, inc=1, device_id={"mp": (q + PLANE * d) % MP}, device_id_type=MESH
        )
        return carry

    def greet_ens(d, carry):
        pl.semaphore_signal(
            barrier, inc=1, device_id={"ens": (e + d) % ENS}, device_id_type=MESH
        )
        return carry

    lax.fori_loop(1, ENS, greet_ens, 0)
    lax.fori_loop(1, PLANES, greet_line, 0)
    lax.fori_loop(1, PLANE, greet_plane, 0)
    pairs = [
        (ens_hbm, ens_v), (ctl_hbm, ctl_v), (band_hbm, band_v), (east_hbm, east_v),
        (north_hbm, north_v), (lon_hbm, lon_v), (inn_hbm, inn_v), (wgt_hbm, wgt_v),
    ]
    loads = [
        pltpu.make_async_copy(src, dst, in_sem.at[n]) for n, (src, dst) in enumerate(pairs)
    ]
    for copy in loads:
        copy.start()

    for ref in (
        sparse_v, fld_v, fldn_s, part_v, state_v, dfull_v, bfull_v, part2_v, state2_v, rows_v
    ):
        ref[...] = jnp.zeros_like(ref)

    source = iota((LON, WIDE), 1)
    embed_v[...] = (
        (iota((LON, WIDE), 0) == (source >> 3) * 6 + (source & 7)) & ((source & 7) < KB)
    ).astype(F32).astype(BF16)
    group = iota((MP, 128), 1) >> 4
    loads[0].wait()
    padded = jnp.dot(ens_v[...], embed_v[...], preferred_element_type=F32)
    ensw_v[...] = padded
    wide_v[...] = jnp.concatenate([padded, jnp.zeros((128 - TILE * LEV, WIDE), F32)], axis=0).T
    by_lon = [wide_v[pl.ds(k, MP, stride=8), :] for k in range(KB)]
    for i in range(TILE):
        block = jnp.zeros((MP, 128), F32)
        for k in range(KB):
            block = jnp.where(group == k, pltpu.roll(by_lon[k], (16 * (k - i)) % 128, 1), block)
        rows_v[pl.ds(i, MP, stride=TILE), :] = block
    a1_send[...] = rows_v[...].reshape(PLANES, PLANE, TILE, 128).astype(BF16)

    pl.semaphore_wait(barrier, PLANE + PLANES + ENS - 3)

    def to_plane(src, middle, n):
        def send(d, carry):
            to = (rank + d) % PLANE
            pltpu.make_async_remote_copy(
                src_ref=src.at[:, to], dst_ref=middle.at[rank],
                send_sem=send_sem.at[n], recv_sem=recv_sem.at[n],
                device_id={"mp": plane * PLANE + to}, device_id_type=MESH,
            ).start()
            return carry

        lax.fori_loop(1, PLANE, send, 0)
        pltpu.make_async_copy(src.at[:, rank], middle.at[rank], recv_sem.at[n]).start()

    def to_line(middle, dst, n):
        for d in range(1, PLANES):
            to = (plane + d) % PLANES
            pltpu.make_async_remote_copy(
                src_ref=middle.at[:, to], dst_ref=dst.at[plane],
                send_sem=send_sem.at[n], recv_sem=recv_sem.at[n],
                device_id={"mp": to * PLANE + rank}, device_id_type=MESH,
            ).start()
        pltpu.make_async_copy(middle.at[:, plane], dst.at[plane], recv_sem.at[n]).start()

    def line_first(src, middle, n):
        for d in range(1, PLANES):
            to = (plane + d) % PLANES
            pltpu.make_async_remote_copy(
                src_ref=src.at[to], dst_ref=middle.at[plane],
                send_sem=send_sem.at[n], recv_sem=recv_sem.at[n],
                device_id={"mp": to * PLANE + rank}, device_id_type=MESH,
            ).start()
        pltpu.make_async_copy(src.at[plane], middle.at[plane], recv_sem.at[n]).start()

    def plane_next(middle, dst, n):
        def send(d, carry):
            to = (rank + d) % PLANE
            pltpu.make_async_remote_copy(
                src_ref=middle.at[:, to], dst_ref=dst.at[:, rank],
                send_sem=send_sem.at[n], recv_sem=recv_sem.at[n],
                device_id={"mp": plane * PLANE + to}, device_id_type=MESH,
            ).start()
            return carry

        lax.fori_loop(1, PLANE, send, 0)
        pltpu.make_async_copy(middle.at[:, rank], dst.at[:, rank], recv_sem.at[n]).start()

    def to_near(src, dst, slots, n):
        for slot, offset in slots:
            pltpu.make_async_remote_copy(
                src_ref=src, dst_ref=dst.at[slot], send_sem=send_sem.at[n],
                recv_sem=recv_sem.at[n],
                device_id={"mp": (q - offset + MP) % MP}, device_id_type=MESH,
            ).start()

    def arrived(ref, n):
        pltpu.make_async_copy(ref, ref, recv_sem.at[n]).wait()

    def sent(ref, n):
        pltpu.make_async_copy(ref, ref, send_sem.at[n]).wait()

    to_plane(a1_send, a1_mid, 0)

    for copy in loads[1:3]:
        copy.wait()
    band = jnp.concatenate([band_v[...].astype(F32), jnp.ones((1, LATP - LAT), F32)], axis=1)
    width_j = jnp.broadcast_to(band, (LATP, LATP))
    width_i = width_j.T
    row, column = iota((LATP, LATP), 0), iota((LATP, LATP), 1)
    distance = jnp.abs(row - column).astype(F32)
    weights = jnp.maximum(0.0, 1.0 - 2.0 * distance / (width_i + width_j))
    kern_v[...] = jnp.where((row < LAT) & (column < LAT), weights, 0.0).astype(BF16)
    spread = jnp.dot(ctl_v[...], kern_v[0:LAT, :], preferred_element_type=F32)
    spread_v[...] = spread.astype(BF16).astype(F32)


    by_tile = lax.dot_general(
        kern_v[0:LAT, 0:LAT], ctl_v[...], (((1,), (1,)), ((), ())), preferred_element_type=F32
    )
    rows_v[...] = jnp.concatenate([by_tile, jnp.zeros((LAT, 128 - KB * LEV), F32)], axis=1)
    by_row = [rows_v[pl.ds(i, MP, stride=TILE), :] for i in range(TILE)]
    for r in range(TILE - 1):
        block = jnp.zeros((MP, 128), F32)
        for h in range(2):
            k = 2 * r + h
            for i in range(TILE):
                moved = pltpu.roll(by_row[i], (64 * h + 16 * (i - k)) % 128, 1)
                block = jnp.where(group == 4 * h + i, moved, block)
        rows_v[pl.ds(r, MP, stride=TILE), :] = block
    for copy in loads[3:5]:
        copy.wait()
    mine = iota((LEV, LON), 0) == e
    winds = []
    for ref in (east_v, north_v):
        for i in range(TILE):
            level = ref[LEV * i : LEV * (i + 1), :].astype(F32)
            winds.append(jnp.sum(jnp.where(mine, level, 0.0), axis=0, keepdims=True))
    wide_winds = jnp.dot(
        jnp.concatenate(winds, axis=0).astype(BF16), embed_v[...], preferred_element_type=F32
    )
    wind_v[...] = wide_winds
    for i in range(TILE):
        sparse_v[0, 16 * i : 16 * i + 1, :] = wide_winds[i : i + 1]
        sparse_v[0, 16 * i + 8 : 16 * i + 9, :] = wide_winds[TILE + i : TILE + i + 1]

    def spaced(at):
        wide_v[...] = sparse_v[at].T
        total = wide_v[pl.ds(0, MP, stride=8), :]
        for k in range(1, KB):
            total = total + pltpu.roll(wide_v[pl.ds(k, MP, stride=8), :], k, 1)
        return total

    rows_v[pl.ds(3, MP, stride=TILE), :] = spaced(0)
    b_send[...] = rows_v[...].reshape(PLANES, PLANE, TILE, 128).astype(BF16)
    line_first(b_send, b_mid, 6)

    for copy in loads[5:]:
        copy.wait()
    own_level = iota((LEV, OBS), 0) == e
    lane_rows = iota((WIDE, OBS), 0)
    places, observed = [], []
    for t in range(SLOTS):
        lon = lon_v[t]
        block = (lon * 10923) >> 16
        place = lon + 2 * block
        places.append(place)
        weight = wgt_v[t]
        level_rows = []
        for i in range(TILE):
            start = LEV * (TILE * t + i)
            level_rows.append(
                jnp.sum(
                    jnp.where(own_level, inn_v[start : start + LEV, :], 0.0),
                    axis=0, keepdims=True,
                )
            )
        level_innovation = jnp.concatenate(level_rows, axis=0)
        observed.append(level_innovation)
        parts = split3(weight) + split3(weight * level_innovation)
        for i in range(TILE):
            hits = (lane_rows == place[i : i + 1, :]).astype(F32).astype(BF16)
            lhs = jnp.concatenate(
                [part[i : i + 1, :] for part in parts] + [jnp.zeros((2, OBS), F32)], axis=0
            ).astype(BF16)
            sums = lax.dot_general(
                lhs, hits, (((1,), (1,)), ((), ())), preferred_element_type=F32
            )
            half, to = 1 + i // 2, 64 * (i % 2) + 8 * t
            sparse_v[half, to : to + 1, :] = sums[0:1] + sums[1:2] + sums[2:3]
            sparse_v[half, to + 32 : to + 33, :] = sums[3:4] + sums[4:5] + sums[5:6]
    for half in range(2):
        pairs_v[pl.ds(half, MP, stride=2), :] = spaced(1 + half)
    f_send[...] = pairs_v[...].reshape(PLANES, PLANE, 2, 128)
    line_first(f_send, f_mid, 1)
    arrived(a1_mid, 0)
    to_line(a1_mid, a1_recv, 8)

    arrived(b_mid, 6)
    plane_next(b_mid, b_recv, 10)
    arrived(f_mid, 1)
    plane_next(f_mid, f_recv, 9)
    arrived(a1_recv, 8)
    gathered = a1_recv[...].astype(F32).reshape(LAT, 128)
    ensk = jnp.concatenate([gathered, jnp.zeros((LATP - LAT, 128), F32)], axis=0).T
    ensk_v[...] = ensk[0 : KB * LEV, :]
    part = ensk[0 : KB * LEV, :] * spread_v[...]
    for k in range(KB):
        for h in range(2):
            part_v[pl.ds(8 * h + k, LEV, stride=16), :] = part[
                LEV * k : LEV * (k + 1), 128 * h : 128 * (h + 1)
            ]

    part_s[...] = part_v[...].reshape(LEV, 16, 128).astype(PART)

    def to_levels(src, dst, n):
        for slot, d in enumerate(LEVEL_ORDER):
            to = (e + d) % ENS
            pltpu.make_async_remote_copy(
                src_ref=src.at[to], dst_ref=dst.at[slot],
                send_sem=send_sem.at[n], recv_sem=recv_sem.at[n],
                device_id={"ens": to}, device_id_type=MESH,
            ).start()

    to_levels(part_s, rs_recv, 4)
    to_near(wind_v, wind_recv, ((0, -1), (1, 1)), 11)

    arrived(b_recv, 10)
    rows_v[...] = b_recv[...].astype(F32).reshape(LAT, 128)
    for r in range(KB // 2):
        block = rows_v[pl.ds(r, MP, stride=TILE), :]
        wide_v[pl.ds(2 * r, MP, stride=8), :] = block
        wide_v[pl.ds(2 * r + 1, MP, stride=8), :] = pltpu.roll(block, 64, 1)
    native = wide_v[...].T
    by_block = rows_v[pl.ds(3, MP, stride=TILE), :]
    for i in range(TILE):
        rows_v[pl.ds(i, MP, stride=TILE), :] = pltpu.roll(by_block, (-16 * i) % 128, 1)
    fields = jnp.concatenate([rows_v[...], jnp.zeros((LATP - LAT, 128), F32)], axis=0).T
    fldw_v[...] = fields[0:16, :]
    fldw_s[...] = fields[0:16, :].astype(BF16)
    to_near(fldw_s, fldw_recv, ((0, -2), (1, -1), (2, 1), (3, 2)), 3)
    for i in range(TILE):
        own = ensw_v[LEV * i : LEV * (i + 1), :] * native[LEV * i : LEV * (i + 1), :]
        for c in range(3):
            part2_v[pl.ds(4 * c + i, LEV, stride=16), :] = own[:, 128 * c : 128 * (c + 1)]
    part2_s[...] = part2_v[...].reshape(LEV, 16, 128).astype(PART2)
    to_levels(part2_s, rs2_recv, 12)

    arrived(f_recv, 9)
    pairs_v[...] = f_recv[...].reshape(2 * MP, 128)
    for half in range(2):
        block = pairs_v[pl.ds(half, MP, stride=2), :]
        rows_v[pl.ds(2 * half, MP, stride=TILE), :] = block
        rows_v[pl.ds(2 * half + 1, MP, stride=TILE), :] = pltpu.roll(block, 64, 1)
    fields = jnp.concatenate([rows_v[...], jnp.zeros((LATP - LAT, 128), F32)], axis=0).T
    fld_v[...] = fields[0:FIELDS, :]
    for t in range(SLOTS):
        n, at = t + 1, t * (t + 1) // 2
        for base, field in ((0, 8 * t), (10, 32 + 8 * t)):
            fldn_s[0, base + at : base + at + n, :] = fld_v[field + KB - n : field + KB, :]
            fldn_s[1, base + at : base + at + n, :] = fld_v[field : field + n, :]
    to_near(fldn_s.at[0], fld_near, ((0, -1),), 2)
    to_near(fldn_s.at[1], fld_near, ((1, 1),), 2)
    arrived(rs_recv, 4)
    total = part_s[e].astype(F32)
    for d in range(ENS - 1):
        total = total + rs_recv[d].astype(F32)
    inc_v[:, 0:128] = total[0:8]
    inc_v[:, 128:256] = total[8:16]
    to_near(inc_v, halo_recv, ((0, -2), (1, -1), (2, 1), (3, 2)), 5)
    arrived(rs2_recv, 12)
    total = part2_s[e].astype(F32)
    for d in range(ENS - 1):
        total = total + rs2_recv[d].astype(F32)
    inc2_v[...] = total
    to_near(inc2_v, halo2_recv, ((0, -1), (1, 1)), 13)
    arrived(fld_near, 2)
    arrived(fldw_recv, 3)
    near = [fldw_recv[n].astype(F32) for n in range(4)]
    inside = (iota((KROWS, LATP), 1) < LAT) & (iota((KROWS, LATP), 0) < 22)
    blank = jnp.zeros((2, LATP), F32)
    winds = []
    for at in (0, 8):
        winds.append(
            jnp.concatenate(
                [
                    near[0][at + 4 : at + 6], near[1][at : at + 6], fldw_v[at : at + 6, :],
                    near[2][at : at + 6], near[3][at : at + 2], blank,
                ],
                axis=0,
            )
        )
    east, north = winds
    coefs = (
        1.0 - jnp.abs(east) - jnp.abs(north),
        jnp.maximum(east, 0.0), jnp.maximum(-east, 0.0),
        jnp.maximum(north, 0.0), jnp.maximum(-north, 0.0),
    )
    for n, coef in enumerate(coefs):
        coef_v[n] = jnp.where(inside, coef, 0.0)
    for t in range(SLOTS):
        n, at = t + 1, t * (t + 1) // 2
        for full, base, field in ((dfull_v, at, 8 * t), (bfull_v, 10 + at, 32 + 8 * t)):
            full[t, 8 - n : 8, :] = fld_near[0, base : base + n, :]
            full[t, 8:14, :] = fld_v[field : field + KB, :]
            full[t, 14 : 14 + n, :] = fld_near[1, base : base + n, :]

    arrived(halo_recv, 5)
    state_v[0, 0:2, :] = halo_recv[0, 4:6, :]
    state_v[0, 2:8, :] = halo_recv[1, 0:6, :]
    state_v[0, 8:14, :] = inc_v[0:6, :]
    state_v[0, 14:20, :] = halo_recv[2, 0:6, :]
    state_v[0, 20:22, :] = halo_recv[3, 0:2, :]

    def west(value):
        return pltpu.roll(value, 1, 0)

    def east_of(value):
        return pltpu.roll(value, KROWS - 1, 0)

    def below(value):
        return pltpu.roll(value, 1, 1)

    def above(value):
        return pltpu.roll(value, LATP - 1, 1)

    center, from_west, from_east, from_south, from_north = [coef_v[n] for n in range(5)]
    quantity = state_v[0]
    for t in range(SLOTS):
        quantity = (
            center * quantity + from_west * west(quantity) + from_east * east_of(quantity)
            + from_south * below(quantity) + from_north * above(quantity)
        )
        state_v[t] = quantity

    sens = jnp.zeros((KROWS, LATP), F32)
    for t in reversed(range(SLOTS)):
        sens = sens + (dfull_v[t] * state_v[t] - bfull_v[t])
        sens = (
            center * sens + east_of(from_west * sens) + west(from_east * sens)
            + above(from_south * sens) + below(from_north * sens)
        )
    own = jnp.concatenate([sens[8:14, :], jnp.zeros((2, LATP), F32)], axis=0)
    ag_send[...] = own.astype(SENS)

    for d in LEVEL_ORDER:
        pltpu.make_async_remote_copy(
            src_ref=ag_send, dst_ref=ag_recv.at[e],
            send_sem=send_sem.at[7], recv_sem=recv_sem.at[7],
            device_id={"ens": (e + d) % ENS}, device_id_type=MESH,
        ).start()
    pltpu.make_async_copy(ag_send, ag_recv.at[e], recv_sem.at[7]).start()

    arrived(wind_recv, 11)
    row = iota((TROWS, WIDE), 0)
    globe = row + (TILE * q - TILE)
    inside = (globe >= 0) & (globe < LAT) & (row < 12)
    slabs = [wind_recv[0], wind_v[...], wind_recv[1]]
    blank = jnp.zeros((TILE, WIDE), F32)
    east = jnp.concatenate([slab[0:4] for slab in slabs] + [blank], axis=0)
    north = jnp.concatenate([slab[4:8] for slab in slabs] + [blank], axis=0)
    coefs = (
        1.0 - jnp.abs(east) - jnp.abs(north),
        jnp.maximum(east, 0.0), jnp.maximum(-east, 0.0),
        jnp.maximum(north, 0.0), jnp.maximum(-north, 0.0),
    )
    for n, coef in enumerate(coefs):
        coef2_v[n] = jnp.where(inside, coef, 0.0)
    arrived(halo2_recv, 13)
    for s in range(3):
        for c in range(3):
            if s == 1:
                piece = inc2_v[4 * c : 4 * c + 4, :]
            else:
                piece = halo2_recv[s // 2, 4 * c : 4 * c + 4, :]
            state2_v[4 * s : 4 * s + 4, 128 * c : 128 * (c + 1)] = piece
    lane = iota((TROWS, WIDE), 1) & 7
    first, last = lane == 0, lane == KB - 1
    center, from_west, from_east, from_south, from_north = [coef2_v[n] for n in range(5)]
    quantity = jnp.where(inside, state2_v[...], 0.0)
    sampled = []
    for t in range(SLOTS):
        quantity = (
            center * quantity
            + from_west
            * jnp.where(first, pltpu.roll(quantity, 3, 1), pltpu.roll(quantity, 1, 1))
            + from_east
            * jnp.where(
                last, pltpu.roll(quantity, WIDE - 3, 1), pltpu.roll(quantity, WIDE - 1, 1)
            )
            + from_south * pltpu.roll(quantity, 1, 0)
            + from_north * pltpu.roll(quantity, TROWS - 1, 0)
        )
        sampled.append(quantity[4:8, :])
    for h in range(2):
        pair = jnp.concatenate(sampled[2 * h : 2 * h + 2], axis=0)
        place = jnp.concatenate(places[2 * h : 2 * h + 2], axis=0)
        value = jnp.zeros((8, OBS), F32)
        for c in range(3):
            picked = jnp.take_along_axis(pair[:, 128 * c : 128 * (c + 1)], place & 127, axis=1)
            value = jnp.where((place >> 7) == c, picked, value)
        dep_v[8 * h : 8 * h + 8, :] = value - jnp.concatenate(observed[2 * h : 2 * h + 2], axis=0)

    sent(a1_mid.at[pl.ds(0, PLANE - 1)], 0)
    sent(a1_recv.at[pl.ds(0, PLANES - 1)], 8)
    for middle, last_ref, n, m in ((b_mid, b_recv, 6, 10), (f_mid, f_recv, 1, 9)):
        sent(middle.at[pl.ds(0, PLANES - 1)], n)
        sent(last_ref.at[:, pl.ds(0, PLANE - 1)], m)
    for ref, n in (
        (fld_near, 2), (fldw_recv, 3), (rs_recv, 4), (halo_recv, 5), (wind_recv, 11),
        (rs2_recv, 12), (halo2_recv, 13),
    ):
        sent(ref, n)

    arrived(ag_recv, 7)
    level_v[...] = ag_recv[...].astype(F32)
    products = jnp.concatenate(
        [
            (ensk_v[LEV * k : LEV * (k + 1), :] * level_v[:, k, :]).astype(BF16).astype(F32)
            for k in range(KB)
        ],
        axis=0,
    ).astype(BF16)
    smooth = jnp.dot(products, kern_v[...], preferred_element_type=F32)
    grad_v[...] = smooth[:, 0:LAT] + ctl_v[...].astype(F32)

    sent(ag_recv.at[pl.ds(0, ENS - 1)], 7)


def move_out(grad_v, dep_v, grad_hbm, dep_hbm, out_sem):
    copies = [
        pltpu.make_async_copy(grad_v, grad_hbm, out_sem.at[0]),
        pltpu.make_async_copy(dep_v, dep_hbm, out_sem.at[1]),
    ]
    for copy in copies:
        copy.start()
    for copy in copies:
        copy.wait()


def shards(
    ensemble, control, band, wind_east, wind_north, observation_longitude, innovation,
    observation_weight,
):
    operands = (
        ensemble.reshape(TILE * LEV, LON),
        jnp.transpose(control, (1, 3, 2, 0)).reshape(KB * LEV, LAT),
        band.reshape(1, LAT),
        wind_east.reshape(TILE * LEV, LON),
        wind_north.reshape(TILE * LEV, LON),
        observation_longitude,
        innovation.reshape(SLOTS * TILE * LEV, OBS),
        observation_weight,
    )
    operands = tuple(pltpu.with_memory_space_constraint(x, pltpu.HBM) for x in operands)
    anywhere = pl.BlockSpec(memory_space=pl.ANY)
    outs = (
        jax.ShapeDtypeStruct((KB * LEV, LAT), F32),
        jax.ShapeDtypeStruct((SLOTS * TILE, OBS), F32),
    )
    scratch = [pltpu.VMEM(x.shape, x.dtype) for x in operands]
    scratch += [
        pltpu.VMEM((LATP, LATP), BF16),
        pltpu.VMEM((LAT, 128), F32),
        pltpu.VMEM((WIDE, 128), F32),
        pltpu.VMEM((KB * LEV, LATP), F32),
        pltpu.VMEM((KB * LEV, LATP), F32),
        pltpu.VMEM((LON, WIDE), BF16),
        pltpu.VMEM((PLANES, PLANE, TILE, 128), BF16),
        pltpu.VMEM((PLANE, PLANES, TILE, 128), BF16),
        pltpu.VMEM((PLANES, PLANE, TILE, 128), BF16),
        pltpu.VMEM((3, 128, WIDE), F32),
        pltpu.VMEM((PLANES, PLANE, 2, 128), F32),
        pltpu.VMEM((PLANES, PLANE, 2, 128), F32),
        pltpu.VMEM((PLANES, PLANE, 2, 128), F32),
        pltpu.VMEM((FIELDS, LATP), F32),
        pltpu.VMEM((2, 24, LATP), F32),
        pltpu.VMEM((2, 24, LATP), F32),
        pltpu.VMEM((16, LATP), F32),
        pltpu.VMEM((16, LATP), BF16),
        pltpu.VMEM((4, 16, LATP), BF16),
        pltpu.VMEM((2 * MP, 128), F32),
        pltpu.VMEM((LEV * 16, 128), F32),
        pltpu.VMEM((LEV, 16, 128), PART),
        pltpu.VMEM((ENS - 1, 16, 128), PART),
        pltpu.VMEM((8, LATP), F32),
        pltpu.VMEM((4, 8, LATP), F32),
        pltpu.VMEM((SLOTS, KROWS, LATP), F32),
        pltpu.VMEM((5, KROWS, LATP), F32),
        pltpu.VMEM((SLOTS, KROWS, LATP), F32),
        pltpu.VMEM((SLOTS, KROWS, LATP), F32),
        pltpu.VMEM((8, LATP), SENS),
        pltpu.VMEM((ENS, 8, LATP), SENS),
        pltpu.VMEM((ENS, 8, LATP), F32),
        pltpu.VMEM((TILE * LEV, WIDE), F32),
        pltpu.VMEM((PLANES, PLANE, TILE, 128), BF16),
        pltpu.VMEM((PLANES, PLANE, TILE, 128), BF16),
        pltpu.VMEM((PLANES, PLANE, TILE, 128), BF16),
        pltpu.VMEM((LEV * 16, 128), F32),
        pltpu.VMEM((LEV, 16, 128), PART2),
        pltpu.VMEM((ENS - 1, 16, 128), PART2),
        pltpu.VMEM((16, 128), F32),
        pltpu.VMEM((2, 16, 128), F32),
        pltpu.VMEM((8, WIDE), F32),
        pltpu.VMEM((2, 8, WIDE), F32),
        pltpu.VMEM((TROWS, WIDE), F32),
        pltpu.VMEM((5, TROWS, WIDE), F32),
        pltpu.SemaphoreType.DMA((8,)),
        pltpu.SemaphoreType.DMA((14,)),
        pltpu.SemaphoreType.DMA((14,)),
    ]
    gradient, departures = pl.pallas_call(
        body,
        out_shape=outs,
        in_specs=[anywhere] * len(operands),
        out_specs=(pl.BlockSpec(memory_space=pltpu.VMEM),) * 2,
        scratch_shapes=scratch,
        compiler_params=pltpu.CompilerParams(
            collective_id=0, has_side_effects=True, vmem_limit_bytes=16 * 1024 * 1024
        ),
        name="assimilate",
    )(*operands)
    gradient, departures = pl.pallas_call(
        move_out,
        out_shape=outs,
        in_specs=[anywhere] * 2,
        out_specs=(pl.BlockSpec(memory_space=pltpu.HBM),) * 2,
        scratch_shapes=[pltpu.SemaphoreType.DMA((2,))],
        compiler_params=pltpu.CompilerParams(vmem_limit_bytes=1024 * 1024),
        name="move_out",
    )(gradient, departures)
    gradient = jnp.transpose(gradient.reshape(1, KB, LEV, LAT), (3, 0, 2, 1))
    return gradient, departures.reshape(SLOTS, TILE, 1, OBS)


def solution(mesh):
    placed = (
        P("mp", "ens", None, None),
        P(None, "ens", None, "mp"),
        P(),
        P("mp", None, None),
        P("mp", None, None),
        P(None, "mp", None),
        P(None, "mp", None, None),
        P(None, "mp", None),
    )
    return jax.shard_map(
        shards,
        mesh=mesh,
        in_specs=placed,
        out_specs=(P(None, "ens", None, "mp"), P(None, "mp", "ens", None)),
        check_vma=False,
    )
```

```python
import jax
import jax.numpy as jnp
from jax import lax
from jax.experimental import pallas as pl
from jax.experimental.pallas import tpu as pltpu
from jax.sharding import PartitionSpec as P

MESH = pl.DeviceIdType.MESH
MP, ENS = 48, 16
PLANES, PLANE = 3, 16
LAT, LEV, LON, OBS, SLOTS = 192, 16, 288, 128, 4
LEVEL_ORDER = (8, 9, 7, 10, 6, 11, 5, 12, 4, 13, 3, 14, 2, 15, 1)
TILE = 4
KB = 6
WIDE = MP * 8
LATP = 256
KROWS = 24
TROWS = 16
PART, PART2 = jnp.bfloat16, jnp.bfloat16
SENS = jnp.bfloat16
FIELDS = 64
F32, BF16 = jnp.float32, jnp.bfloat16


def iota(shape, dim):
    return lax.broadcasted_iota(jnp.int32, shape, dim)


def split3(value):
    first = value.astype(BF16)
    rest = value - first.astype(F32)
    second = rest.astype(BF16)
    third = (rest - second.astype(F32)).astype(BF16)
    return first.astype(F32), second.astype(F32), third.astype(F32)


def body(
    ens_hbm, ctl_hbm, band_hbm, east_hbm, north_hbm, lon_hbm, inn_hbm, wgt_hbm,
    grad_v, dep_v,
    ens_v, ctl_v, band_v, east_v, north_v, lon_v, inn_v, wgt_v,
    kern_v, rows_v, wide_v, spread_v, ensk_v, embed_v,
    a1_send, a1_mid, a1_recv, sparse_v, f_send, f_mid, f_recv, fld_v, edge_v, fldn_s, fld_near, fldw_v, fldw_s, fldw_recv, pairs_v,
    part_v, part_s, rs_recv, inc_v, halo_recv, inc_far_s, halo_far, state_v, coef_v, dfull_v, bfull_v,
    ag_send, ag_recv, level_v,
    ensw_v, b_send, b_mid, b_recv, part2_v, part2_s, rs2_recv, inc2_v, halo2_recv,
    wind_v, wind_s, wind_recv, state2_v, coef2_v,
    in_sem, send_sem, recv_sem,
):
    q = lax.axis_index("mp")
    e = lax.axis_index("ens")
    plane, rank = q // PLANE, q % PLANE

    barrier = pltpu.get_barrier_semaphore()

    def greet(device):
        pl.semaphore_signal(barrier, inc=1, device_id=device, device_id_type=MESH)

    for d in LEVEL_ORDER:
        greet({"ens": (e + d) % ENS})
    for d in range(1, PLANES):
        greet({"mp": (q + PLANE * d) % MP})
    for d in LEVEL_ORDER:
        greet({"mp": plane * PLANE + (rank + d) % PLANE})
    pairs = [
        (ens_hbm, ens_v), (ctl_hbm, ctl_v), (band_hbm, band_v), (east_hbm, east_v),
        (north_hbm, north_v), (lon_hbm, lon_v), (inn_hbm, inn_v), (wgt_hbm, wgt_v),
    ]
    loads = [
        pltpu.make_async_copy(src, dst, in_sem.at[n]) for n, (src, dst) in enumerate(pairs)
    ]
    for copy in loads:
        copy.start()

    for ref in (
        sparse_v, fld_v, fldn_s, part_v, state_v, dfull_v, bfull_v, part2_v, state2_v, rows_v
    ):
        ref[...] = jnp.zeros_like(ref)

    source = iota((LON, WIDE), 1)
    embed_v[...] = (
        (iota((LON, WIDE), 0) == (source >> 3) * 6 + (source & 7)) & ((source & 7) < KB)
    ).astype(F32).astype(BF16)
    group = iota((MP, 128), 1) >> 4
    loads[0].wait()
    padded = jnp.dot(ens_v[...], embed_v[...], preferred_element_type=F32)
    ensw_v[...] = padded
    wide_v[...] = jnp.concatenate([padded, jnp.zeros((128 - TILE * LEV, WIDE), F32)], axis=0).T
    by_lon = [wide_v[pl.ds(k, MP, stride=8), :] for k in range(KB)]
    for copy in loads[3:5]:
        copy.wait()
    mine = iota((LEV, LON), 0) == e
    winds = []
    for ref in (east_v, north_v):
        for i in range(TILE):
            level = ref[LEV * i : LEV * (i + 1), :].astype(F32)
            winds.append(jnp.sum(jnp.where(mine, level, 0.0), axis=0, keepdims=True))
    wide_winds = jnp.dot(
        jnp.concatenate(winds, axis=0).astype(BF16), embed_v[...], preferred_element_type=F32
    )
    wind_v[...] = wide_winds
    wind_s[...] = wide_winds.astype(BF16)
    for i in range(TILE):
        sparse_v[0, 16 * i : 16 * i + 1, :] = wide_winds[i : i + 1]
        sparse_v[0, 16 * i + 8 : 16 * i + 9, :] = wide_winds[TILE + i : TILE + i + 1]

    def spaced(at):
        wide_v[...] = sparse_v[at].T
        total = wide_v[pl.ds(0, MP, stride=8), :]
        for k in range(1, KB):
            total = total + pltpu.roll(wide_v[pl.ds(k, MP, stride=8), :], k, 1)
        return total

    wind_lanes = spaced(0)
    for i in range(TILE):
        block = jnp.where(group == 6, pltpu.roll(wind_lanes, (96 - 16 * i) % 128, 1), 0.0)
        for k in range(KB):
            block = jnp.where(group == k, pltpu.roll(by_lon[k], (16 * (k - i)) % 128, 1), block)
        rows_v[pl.ds(i, MP, stride=TILE), :] = block
    a1_send[...] = rows_v[...].reshape(PLANES, PLANE, TILE, 128).astype(BF16)

    for copy in loads[5:]:
        copy.wait()
    own_level = iota((LEV, OBS), 0) == e
    lane_rows = iota((WIDE, OBS), 0)
    places, observed = [], []
    for t in range(SLOTS):
        lon = lon_v[t]
        block = (lon * 10923) >> 16
        place = lon + 2 * block
        places.append(place)
        weight = wgt_v[t]
        level_rows = []
        for i in range(TILE):
            start = LEV * (TILE * t + i)
            level_rows.append(
                jnp.sum(
                    jnp.where(own_level, inn_v[start : start + LEV, :], 0.0),
                    axis=0, keepdims=True,
                )
            )
        level_innovation = jnp.concatenate(level_rows, axis=0)
        observed.append(level_innovation)
        parts = split3(weight) + split3(weight * level_innovation)
        for i in range(TILE):
            hits = (lane_rows == place[i : i + 1, :]).astype(F32).astype(BF16)
            lhs = jnp.concatenate(
                [part[i : i + 1, :] for part in parts] + [jnp.zeros((2, OBS), F32)], axis=0
            ).astype(BF16)
            sums = lax.dot_general(
                lhs, hits, (((1,), (1,)), ((), ())), preferred_element_type=F32
            )
            half, to = 1 + i // 2, 64 * (i % 2) + 8 * t
            sparse_v[half, to : to + 1, :] = sums[0:1] + sums[1:2] + sums[2:3]
            sparse_v[half, to + 32 : to + 33, :] = sums[3:4] + sums[4:5] + sums[5:6]
    for half in range(2):
        pairs_v[pl.ds(half, MP, stride=2), :] = spaced(1 + half)
    f_send[...] = pairs_v[...].reshape(PLANES, PLANE, 2, 128)
    pl.semaphore_wait(barrier, PLANE + PLANES + ENS - 3)

    def to_plane(src, middle, n):
        for d in LEVEL_ORDER:
            to = (rank + d) % PLANE
            pltpu.make_async_remote_copy(
                src_ref=src.at[:, to], dst_ref=middle.at[rank],
                send_sem=send_sem.at[n], recv_sem=recv_sem.at[n],
                device_id={"mp": plane * PLANE + to}, device_id_type=MESH,
            ).start()
        pltpu.make_async_copy(src.at[:, rank], middle.at[rank], recv_sem.at[n]).start()

    def to_line(middle, dst, n):
        for d in range(1, PLANES):
            to = (plane + d) % PLANES
            pltpu.make_async_remote_copy(
                src_ref=middle.at[:, to], dst_ref=dst.at[plane],
                send_sem=send_sem.at[n], recv_sem=recv_sem.at[n],
                device_id={"mp": to * PLANE + rank}, device_id_type=MESH,
            ).start()
        pltpu.make_async_copy(middle.at[:, plane], dst.at[plane], recv_sem.at[n]).start()

    def line_first(src, middle, n):
        for d in range(1, PLANES):
            to = (plane + d) % PLANES
            pltpu.make_async_remote_copy(
                src_ref=src.at[to], dst_ref=middle.at[plane],
                send_sem=send_sem.at[n], recv_sem=recv_sem.at[n],
                device_id={"mp": to * PLANE + rank}, device_id_type=MESH,
            ).start()
        pltpu.make_async_copy(src.at[plane], middle.at[plane], recv_sem.at[n]).start()

    def plane_next(middle, dst, n):
        def send(d, carry):
            to = (rank + d) % PLANE
            pltpu.make_async_remote_copy(
                src_ref=middle.at[:, to], dst_ref=dst.at[:, rank],
                send_sem=send_sem.at[n], recv_sem=recv_sem.at[n],
                device_id={"mp": plane * PLANE + to}, device_id_type=MESH,
            ).start()
            return carry

        lax.fori_loop(1, PLANE, send, 0)
        pltpu.make_async_copy(middle.at[:, rank], dst.at[:, rank], recv_sem.at[n]).start()

    def to_near(src, dst, slots, n):
        for slot, offset in slots:
            pltpu.make_async_remote_copy(
                src_ref=src, dst_ref=dst.at[slot], send_sem=send_sem.at[n],
                recv_sem=recv_sem.at[n],
                device_id={"mp": (q - offset + MP) % MP}, device_id_type=MESH,
            ).start()

    def arrived(ref, n):
        pltpu.make_async_copy(ref, ref, recv_sem.at[n]).wait()

    def sent(ref, n):
        pltpu.make_async_copy(ref, ref, send_sem.at[n]).wait()

    to_plane(a1_send, a1_mid, 0)
    line_first(f_send, f_mid, 1)

    for copy in loads[1:3]:
        copy.wait()
    band = jnp.concatenate([band_v[...].astype(F32), jnp.ones((1, LATP - LAT), F32)], axis=1)
    width_j = jnp.broadcast_to(band, (LATP, LATP))
    width_i = width_j.T
    row, column = iota((LATP, LATP), 0), iota((LATP, LATP), 1)
    distance = jnp.abs(row - column).astype(F32)
    weights = jnp.maximum(0.0, 1.0 - 2.0 * distance / (width_i + width_j))
    kern_v[...] = jnp.where((row < LAT) & (column < LAT), weights, 0.0).astype(BF16)
    spread = jnp.dot(ctl_v[...], kern_v[0:LAT, :], preferred_element_type=F32)
    spread_v[...] = spread.astype(BF16).astype(F32)


    by_tile = lax.dot_general(
        kern_v[0:LAT, 0:LAT], ctl_v[...], (((1,), (1,)), ((), ())), preferred_element_type=F32
    )
    rows_v[...] = jnp.concatenate([by_tile, jnp.zeros((LAT, 128 - KB * LEV), F32)], axis=1)
    by_row = [rows_v[pl.ds(i, MP, stride=TILE), :] for i in range(TILE)]
    for r in range(TILE - 1):
        block = jnp.zeros((MP, 128), F32)
        for h in range(2):
            k = 2 * r + h
            for i in range(TILE):
                moved = pltpu.roll(by_row[i], (64 * h + 16 * (i - k)) % 128, 1)
                block = jnp.where(group == 4 * h + i, moved, block)
        rows_v[pl.ds(r, MP, stride=TILE), :] = block
    b_send[...] = rows_v[...].reshape(PLANES, PLANE, TILE, 128).astype(BF16)
    line_first(b_send, b_mid, 6)


    arrived(a1_mid, 0)
    to_line(a1_mid, a1_recv, 8)
    arrived(f_mid, 1)
    plane_next(f_mid, f_recv, 9)
    arrived(b_mid, 6)
    plane_next(b_mid, b_recv, 10)
    arrived(a1_recv, 8)
    gathered = a1_recv[...].astype(F32).reshape(LAT, 128)
    ensk = jnp.concatenate([gathered, jnp.zeros((LATP - LAT, 128), F32)], axis=0).T
    ensk_v[...] = ensk[0 : KB * LEV, :]
    part = ensk[0 : KB * LEV, :] * spread_v[...]
    for k in range(KB):
        for h in range(2):
            part_v[pl.ds(8 * h + k, LEV, stride=16), :] = part[
                LEV * k : LEV * (k + 1), 128 * h : 128 * (h + 1)
            ]

    part_s[...] = part_v[...].reshape(LEV, 16, 128).astype(PART)

    def to_levels(src, dst, n):
        for slot, d in enumerate(LEVEL_ORDER):
            to = (e + d) % ENS
            pltpu.make_async_remote_copy(
                src_ref=src.at[to], dst_ref=dst.at[slot],
                send_sem=send_sem.at[n], recv_sem=recv_sem.at[n],
                device_id={"ens": to}, device_id_type=MESH,
            ).start()

    to_levels(part_s, rs_recv, 4)
    fldw_v[...] = ensk[96:112, :]
    fldw_s[...] = ensk[96:112, :].astype(BF16)
    to_near(fldw_s, fldw_recv, ((0, -2), (1, -1), (2, 1), (3, 2)), 3)
    to_near(wind_s, wind_recv, ((0, -1), (1, 1)), 11)

    arrived(f_recv, 9)
    pairs_v[...] = f_recv[...].reshape(2 * MP, 128)
    for half in range(2):
        block = pairs_v[pl.ds(half, MP, stride=2), :]
        rows_v[pl.ds(2 * half, MP, stride=TILE), :] = block
        rows_v[pl.ds(2 * half + 1, MP, stride=TILE), :] = pltpu.roll(block, 64, 1)
    fields = jnp.concatenate([rows_v[...], jnp.zeros((LATP - LAT, 128), F32)], axis=0).T
    fld_v[...] = fields[0:FIELDS, :]
    for t in range(SLOTS):
        n, at = t + 1, t * (t + 1) // 2
        for base, field in ((0, 8 * t), (10, 32 + 8 * t)):
            edge_v[0, base + at : base + at + n, :] = fld_v[field + KB - n : field + KB, :]
            edge_v[1, base + at : base + at + n, :] = fld_v[field : field + n, :]
    for side in range(2):
        fldn_s[side, 0:20, :] = edge_v[side, 0:20, 0:128]
        fldn_s[side, 20:30, :] = edge_v[side, 0:10, 128:256] + pltpu.roll(
            edge_v[side, 10:20, 128:256], 64, 1
        )
    to_near(fldn_s.at[0], fld_near, ((0, -1),), 2)
    to_near(fldn_s.at[1], fld_near, ((1, 1),), 2)
    arrived(b_recv, 10)
    rows_v[...] = b_recv[...].astype(F32).reshape(LAT, 128)
    for r in range(KB // 2):
        block = rows_v[pl.ds(r, MP, stride=TILE), :]
        wide_v[pl.ds(2 * r, MP, stride=8), :] = block
        wide_v[pl.ds(2 * r + 1, MP, stride=8), :] = pltpu.roll(block, 64, 1)
    native = wide_v[...].T
    for i in range(TILE):
        own = ensw_v[LEV * i : LEV * (i + 1), :] * native[LEV * i : LEV * (i + 1), :]
        for c in range(3):
            part2_v[pl.ds(4 * c + i, LEV, stride=16), :] = own[:, 128 * c : 128 * (c + 1)]
    part2_s[...] = part2_v[...].reshape(LEV, 16, 128).astype(PART2)
    to_levels(part2_s, rs2_recv, 12)

    arrived(rs_recv, 4)
    total = part_s[e].astype(F32)
    for d in range(ENS - 1):
        total = total + rs_recv[d].astype(F32)
    inc_v[:, 0:128] = total[0:8]
    inc_v[:, 128:256] = total[8:16]
    inc_far_s[0] = inc_v[4:6, :]
    inc_far_s[1] = inc_v[0:2, :]
    to_near(inc_v, halo_recv, ((0, -1), (1, 1)), 5)
    to_near(inc_far_s.at[0], halo_far, ((0, -2),), 14)
    to_near(inc_far_s.at[1], halo_far, ((1, 2),), 14)
    arrived(rs2_recv, 12)
    total = part2_s[e].astype(F32)
    for d in range(ENS - 1):
        total = total + rs2_recv[d].astype(F32)
    inc2_v[...] = total
    to_near(inc2_v, halo2_recv, ((0, -1), (1, 1)), 13)
    arrived(fld_near, 2)
    arrived(fldw_recv, 3)
    near = [fldw_recv[n].astype(F32) for n in range(4)]
    low_half = iota((10, 128), 1) < 64
    for side in range(2):
        rest = fld_near[side, 20:30, :]
        edge_v[side, 0:20, 0:128] = fld_near[side, 0:20, :]
        edge_v[side, 0:10, 128:256] = jnp.where(low_half, rest, 0.0)
        edge_v[side, 10:20, 128:256] = jnp.where(low_half, pltpu.roll(rest, 64, 1), 0.0)
    inside = (iota((KROWS, LATP), 1) < LAT) & (iota((KROWS, LATP), 0) < 22)
    blank = jnp.zeros((2, LATP), F32)
    winds = []
    for at in (0, 8):
        winds.append(
            jnp.concatenate(
                [
                    near[0][at + 4 : at + 6], near[1][at : at + 6], fldw_v[at : at + 6, :],
                    near[2][at : at + 6], near[3][at : at + 2], blank,
                ],
                axis=0,
            )
        )
    east, north = winds
    coefs = (
        1.0 - jnp.abs(east) - jnp.abs(north),
        jnp.maximum(east, 0.0), jnp.maximum(-east, 0.0),
        jnp.maximum(north, 0.0), jnp.maximum(-north, 0.0),
    )
    for n, coef in enumerate(coefs):
        coef_v[n] = jnp.where(inside, coef, 0.0)
    for t in range(SLOTS):
        n, at = t + 1, t * (t + 1) // 2
        for full, base, field in ((dfull_v, at, 8 * t), (bfull_v, 10 + at, 32 + 8 * t)):
            full[t, 8 - n : 8, :] = edge_v[0, base : base + n, :]
            full[t, 8:14, :] = fld_v[field : field + KB, :]
            full[t, 14 : 14 + n, :] = edge_v[1, base : base + n, :]

    state_v[0, 8:14, :] = inc_v[0:6, :]
    arrived(halo_recv, 5)
    arrived(halo_far, 14)
    state_v[0, 0:2, :] = halo_far[0]
    state_v[0, 2:8, :] = halo_recv[0, 0:6, :]
    state_v[0, 14:20, :] = halo_recv[1, 0:6, :]
    state_v[0, 20:22, :] = halo_far[1]

    def west(value):
        return pltpu.roll(value, 1, 0)

    def east_of(value):
        return pltpu.roll(value, KROWS - 1, 0)

    def below(value):
        return pltpu.roll(value, 1, 1)

    def above(value):
        return pltpu.roll(value, LATP - 1, 1)

    center, from_west, from_east, from_south, from_north = [coef_v[n] for n in range(5)]
    quantity = state_v[0]
    for t in range(SLOTS):
        quantity = (
            center * quantity + from_west * west(quantity) + from_east * east_of(quantity)
            + from_south * below(quantity) + from_north * above(quantity)
        )
        state_v[t] = quantity

    sens = jnp.zeros((KROWS, LATP), F32)
    for t in reversed(range(SLOTS)):
        sens = sens + (dfull_v[t] * state_v[t] - bfull_v[t])
        sens = (
            center * sens + east_of(from_west * sens) + west(from_east * sens)
            + above(from_south * sens) + below(from_north * sens)
        )
    own = jnp.concatenate([sens[8:14, :], jnp.zeros((2, LATP), F32)], axis=0)
    ag_send[...] = own.astype(SENS)

    for d in LEVEL_ORDER:
        pltpu.make_async_remote_copy(
            src_ref=ag_send, dst_ref=ag_recv.at[e],
            send_sem=send_sem.at[7], recv_sem=recv_sem.at[7],
            device_id={"ens": (e + d) % ENS}, device_id_type=MESH,
        ).start()
    pltpu.make_async_copy(ag_send, ag_recv.at[e], recv_sem.at[7]).start()

    arrived(wind_recv, 11)
    row = iota((TROWS, WIDE), 0)
    globe = row + (TILE * q - TILE)
    inside = (globe >= 0) & (globe < LAT) & (row < 12)
    slabs = [wind_recv[0].astype(F32), wind_v[...], wind_recv[1].astype(F32)]
    blank = jnp.zeros((TILE, WIDE), F32)
    east = jnp.concatenate([slab[0:4] for slab in slabs] + [blank], axis=0)
    north = jnp.concatenate([slab[4:8] for slab in slabs] + [blank], axis=0)
    coefs = (
        1.0 - jnp.abs(east) - jnp.abs(north),
        jnp.maximum(east, 0.0), jnp.maximum(-east, 0.0),
        jnp.maximum(north, 0.0), jnp.maximum(-north, 0.0),
    )
    for n, coef in enumerate(coefs):
        coef2_v[n] = jnp.where(inside, coef, 0.0)
    arrived(halo2_recv, 13)
    for s in range(3):
        for c in range(3):
            if s == 1:
                piece = inc2_v[4 * c : 4 * c + 4, :]
            else:
                piece = halo2_recv[s // 2, 4 * c : 4 * c + 4, :]
            state2_v[4 * s : 4 * s + 4, 128 * c : 128 * (c + 1)] = piece
    lane = iota((TROWS, WIDE), 1) & 7
    first, last = lane == 0, lane == KB - 1
    center, from_west, from_east, from_south, from_north = [coef2_v[n] for n in range(5)]
    quantity = jnp.where(inside, state2_v[...], 0.0)
    sampled = []
    for t in range(SLOTS):
        quantity = (
            center * quantity
            + from_west
            * jnp.where(first, pltpu.roll(quantity, 3, 1), pltpu.roll(quantity, 1, 1))
            + from_east
            * jnp.where(
                last, pltpu.roll(quantity, WIDE - 3, 1), pltpu.roll(quantity, WIDE - 1, 1)
            )
            + from_south * pltpu.roll(quantity, 1, 0)
            + from_north * pltpu.roll(quantity, TROWS - 1, 0)
        )
        sampled.append(quantity[4:8, :])
    for h in range(2):
        pair = jnp.concatenate(sampled[2 * h : 2 * h + 2], axis=0)
        place = jnp.concatenate(places[2 * h : 2 * h + 2], axis=0)
        value = jnp.zeros((8, OBS), F32)
        for c in range(3):
            picked = jnp.take_along_axis(pair[:, 128 * c : 128 * (c + 1)], place & 127, axis=1)
            value = jnp.where((place >> 7) == c, picked, value)
        dep_v[8 * h : 8 * h + 8, :] = value - jnp.concatenate(observed[2 * h : 2 * h + 2], axis=0)

    sent(a1_mid.at[pl.ds(0, PLANE - 1)], 0)
    sent(a1_recv.at[pl.ds(0, PLANES - 1)], 8)
    for middle, last_ref, n, m in ((b_mid, b_recv, 6, 10), (f_mid, f_recv, 1, 9)):
        sent(middle.at[pl.ds(0, PLANES - 1)], n)
        sent(last_ref.at[:, pl.ds(0, PLANE - 1)], m)
    for ref, n in (
        (fld_near, 2), (fldw_recv, 3), (rs_recv, 4), (halo_recv, 5), (wind_recv, 11),
        (rs2_recv, 12), (halo2_recv, 13), (halo_far, 14),
    ):
        sent(ref, n)

    arrived(ag_recv, 7)
    level_v[...] = ag_recv[...].astype(F32)
    products = jnp.concatenate(
        [
            (ensk_v[LEV * k : LEV * (k + 1), :] * level_v[:, k, :]).astype(BF16).astype(F32)
            for k in range(KB)
        ],
        axis=0,
    ).astype(BF16)
    smooth = jnp.dot(products, kern_v[...], preferred_element_type=F32)
    grad_v[...] = smooth[:, 0:LAT] + ctl_v[...].astype(F32)

    sent(ag_recv.at[pl.ds(0, ENS - 1)], 7)


def move_out(grad_v, dep_v, grad_hbm, dep_hbm, out_sem):
    copies = [
        pltpu.make_async_copy(grad_v, grad_hbm, out_sem.at[0]),
        pltpu.make_async_copy(dep_v, dep_hbm, out_sem.at[1]),
    ]
    for copy in copies:
        copy.start()
    for copy in copies:
        copy.wait()


def shards(
    ensemble, control, band, wind_east, wind_north, observation_longitude, innovation,
    observation_weight,
):
    operands = (
        ensemble.reshape(TILE * LEV, LON),
        jnp.transpose(control, (1, 3, 2, 0)).reshape(KB * LEV, LAT),
        band.reshape(1, LAT),
        wind_east.reshape(TILE * LEV, LON),
        wind_north.reshape(TILE * LEV, LON),
        observation_longitude,
        innovation.reshape(SLOTS * TILE * LEV, OBS),
        observation_weight,
    )
    operands = tuple(pltpu.with_memory_space_constraint(x, pltpu.HBM) for x in operands)
    anywhere = pl.BlockSpec(memory_space=pl.ANY)
    outs = (
        jax.ShapeDtypeStruct((KB * LEV, LAT), F32),
        jax.ShapeDtypeStruct((SLOTS * TILE, OBS), F32),
    )
    scratch = [pltpu.VMEM(x.shape, x.dtype) for x in operands]
    scratch += [
        pltpu.VMEM((LATP, LATP), BF16),
        pltpu.VMEM((LAT, 128), F32),
        pltpu.VMEM((WIDE, 128), F32),
        pltpu.VMEM((KB * LEV, LATP), F32),
        pltpu.VMEM((KB * LEV, LATP), F32),
        pltpu.VMEM((LON, WIDE), BF16),
        pltpu.VMEM((PLANES, PLANE, TILE, 128), BF16),
        pltpu.VMEM((PLANE, PLANES, TILE, 128), BF16),
        pltpu.VMEM((PLANES, PLANE, TILE, 128), BF16),
        pltpu.VMEM((3, 128, WIDE), F32),
        pltpu.VMEM((PLANES, PLANE, 2, 128), F32),
        pltpu.VMEM((PLANES, PLANE, 2, 128), F32),
        pltpu.VMEM((PLANES, PLANE, 2, 128), F32),
        pltpu.VMEM((FIELDS, LATP), F32),
        pltpu.VMEM((2, 24, LATP), F32),
        pltpu.VMEM((2, 32, 128), F32),
        pltpu.VMEM((2, 32, 128), F32),
        pltpu.VMEM((16, LATP), F32),
        pltpu.VMEM((16, LATP), BF16),
        pltpu.VMEM((4, 16, LATP), BF16),
        pltpu.VMEM((2 * MP, 128), F32),
        pltpu.VMEM((LEV * 16, 128), F32),
        pltpu.VMEM((LEV, 16, 128), PART),
        pltpu.VMEM((ENS - 1, 16, 128), PART),
        pltpu.VMEM((8, LATP), F32),
        pltpu.VMEM((2, 8, LATP), F32),
        pltpu.VMEM((2, 2, LATP), F32),
        pltpu.VMEM((2, 2, LATP), F32),
        pltpu.VMEM((SLOTS, KROWS, LATP), F32),
        pltpu.VMEM((5, KROWS, LATP), F32),
        pltpu.VMEM((SLOTS, KROWS, LATP), F32),
        pltpu.VMEM((SLOTS, KROWS, LATP), F32),
        pltpu.VMEM((8, LATP), SENS),
        pltpu.VMEM((ENS, 8, LATP), SENS),
        pltpu.VMEM((ENS, 8, LATP), F32),
        pltpu.VMEM((TILE * LEV, WIDE), F32),
        pltpu.VMEM((PLANES, PLANE, TILE, 128), BF16),
        pltpu.VMEM((PLANES, PLANE, TILE, 128), BF16),
        pltpu.VMEM((PLANES, PLANE, TILE, 128), BF16),
        pltpu.VMEM((LEV * 16, 128), F32),
        pltpu.VMEM((LEV, 16, 128), PART2),
        pltpu.VMEM((ENS - 1, 16, 128), PART2),
        pltpu.VMEM((16, 128), F32),
        pltpu.VMEM((2, 16, 128), F32),
        pltpu.VMEM((8, WIDE), F32),
        pltpu.VMEM((8, WIDE), BF16),
        pltpu.VMEM((2, 8, WIDE), BF16),
        pltpu.VMEM((TROWS, WIDE), F32),
        pltpu.VMEM((5, TROWS, WIDE), F32),
        pltpu.SemaphoreType.DMA((8,)),
        pltpu.SemaphoreType.DMA((15,)),
        pltpu.SemaphoreType.DMA((15,)),
    ]
    gradient, departures = pl.pallas_call(
        body,
        out_shape=outs,
        in_specs=[anywhere] * len(operands),
        out_specs=(pl.BlockSpec(memory_space=pltpu.VMEM),) * 2,
        scratch_shapes=scratch,
        compiler_params=pltpu.CompilerParams(
            collective_id=0, has_side_effects=True, vmem_limit_bytes=16 * 1024 * 1024
        ),
        name="assimilate",
    )(*operands)
    gradient, departures = pl.pallas_call(
        move_out,
        out_shape=outs,
        in_specs=[anywhere] * 2,
        out_specs=(pl.BlockSpec(memory_space=pltpu.HBM),) * 2,
        scratch_shapes=[pltpu.SemaphoreType.DMA((2,))],
        compiler_params=pltpu.CompilerParams(vmem_limit_bytes=1024 * 1024),
        name="move_out",
    )(gradient, departures)
    gradient = jnp.transpose(gradient.reshape(1, KB, LEV, LAT), (3, 0, 2, 1))
    return gradient, departures.reshape(SLOTS, TILE, 1, OBS)


def solution(mesh):
    placed = (
        P("mp", "ens", None, None),
        P(None, "ens", None, "mp"),
        P(),
        P("mp", None, None),
        P("mp", None, None),
        P(None, "mp", None),
        P(None, "mp", None, None),
        P(None, "mp", None),
    )
    return jax.shard_map(
        shards,
        mesh=mesh,
        in_specs=placed,
        out_specs=(P(None, "ens", None, "mp"), P(None, "mp", "ens", None)),
        check_vma=False,
    )
```

```python
import jax
import jax.numpy as jnp
from jax import lax
from jax.experimental import pallas as pl
from jax.experimental.pallas import tpu as pltpu
from jax.sharding import PartitionSpec as P

MESH = pl.DeviceIdType.MESH
MP, ENS = 48, 16
PLANES, PLANE = 3, 16
LAT, LEV, LON, OBS, SLOTS = 192, 16, 288, 128, 4
LEVEL_ORDER = (8, 9, 7, 10, 6, 11, 5, 12, 4, 13, 3, 14, 2, 15, 1)
TILE = 4
KB = 6
WIDE = MP * 8
LATP = 256
KROWS = 24
TROWS = 16
PART, PART2 = jnp.bfloat16, jnp.bfloat16
SENS = jnp.bfloat16
FIELDS = 64
F32, BF16 = jnp.float32, jnp.bfloat16


def iota(shape, dim):
    return lax.broadcasted_iota(jnp.int32, shape, dim)


def split3(value):
    first = value.astype(BF16)
    rest = value - first.astype(F32)
    second = rest.astype(BF16)
    third = (rest - second.astype(F32)).astype(BF16)
    return first.astype(F32), second.astype(F32), third.astype(F32)


def body(
    ens_hbm, ctl_hbm, band_hbm, east_hbm, north_hbm, lon_hbm, inn_hbm, wgt_hbm,
    grad_v, dep_v,
    ens_v, ctl_v, band_v, east_v, north_v, lon_v, inn_v, wgt_v,
    kern_v, rows_v, wide_v, spread_v, ensk_v, embed_v,
    a1_send, a1_mid, a1_recv, sparse_v, f_send, f_mid, f_recv, fld_v, edge_v, fldn_s, fld_near, fldw_v, fldw_s, fldw_recv, pairs_v,
    part_v, part_s, rs_recv, inc_v, halo_recv, inc_far_s, halo_far, state_v, coef_v, dfull_v, bfull_v,
    ag_send, ag_recv, level_v,
    ensw_v, b_send, b_mid, b_recv, part2_v, part2_s, rs2_recv, inc2_v, halo2_recv,
    wind_v, wind_s, wind_recv, state2_v, coef2_v,
    in_sem, send_sem, recv_sem,
):
    q = lax.axis_index("mp")
    e = lax.axis_index("ens")
    plane, rank = q // PLANE, q % PLANE

    barrier = pltpu.get_barrier_semaphore()

    def greet(device):
        pl.semaphore_signal(barrier, inc=1, device_id=device, device_id_type=MESH)

    for d in LEVEL_ORDER:
        greet({"ens": (e + d) % ENS})
    for d in range(1, PLANES):
        greet({"mp": (q + PLANE * d) % MP})
    for d in LEVEL_ORDER:
        greet({"mp": plane * PLANE + (rank + d) % PLANE})
    pairs = [
        (ens_hbm, ens_v), (ctl_hbm, ctl_v), (band_hbm, band_v), (east_hbm, east_v),
        (north_hbm, north_v), (lon_hbm, lon_v), (inn_hbm, inn_v), (wgt_hbm, wgt_v),
    ]
    loads = [
        pltpu.make_async_copy(src, dst, in_sem.at[(0, 1, 1, 2, 2, 3, 3, 3)[n]])
        for n, (src, dst) in enumerate(pairs)
    ]
    for copy in loads:
        copy.start()

    for ref in (
        sparse_v, fld_v, fldn_s, part_v, state_v, dfull_v, bfull_v, part2_v, state2_v, rows_v
    ):
        ref[...] = jnp.zeros_like(ref)

    source = iota((LON, WIDE), 1)
    embed_v[...] = (
        (iota((LON, WIDE), 0) == (source >> 3) * 6 + (source & 7)) & ((source & 7) < KB)
    ).astype(F32).astype(BF16)
    group = iota((MP, 128), 1) >> 4
    loads[0].wait()
    padded = jnp.dot(ens_v[...], embed_v[...], preferred_element_type=F32)
    ensw_v[...] = padded
    wide_v[...] = jnp.concatenate([padded, jnp.zeros((128 - TILE * LEV, WIDE), F32)], axis=0).T
    by_lon = [wide_v[pl.ds(k, MP, stride=8), :] for k in range(KB)]
    for copy in loads[3:5]:
        copy.wait()
    mine = iota((LEV, LON), 0) == e
    winds = []
    for ref in (east_v, north_v):
        for i in range(TILE):
            level = ref[LEV * i : LEV * (i + 1), :].astype(F32)
            winds.append(jnp.sum(jnp.where(mine, level, 0.0), axis=0, keepdims=True))
    wide_winds = jnp.dot(
        jnp.concatenate(winds, axis=0).astype(BF16), embed_v[...], preferred_element_type=F32
    )
    wind_v[...] = wide_winds
    wind_s[...] = wide_winds.astype(BF16)
    for i in range(TILE):
        sparse_v[0, 16 * i : 16 * i + 1, :] = wide_winds[i : i + 1]
        sparse_v[0, 16 * i + 8 : 16 * i + 9, :] = wide_winds[TILE + i : TILE + i + 1]

    def spaced(at):
        wide_v[...] = sparse_v[at].T
        total = wide_v[pl.ds(0, MP, stride=8), :]
        for k in range(1, KB):
            total = total + pltpu.roll(wide_v[pl.ds(k, MP, stride=8), :], k, 1)
        return total

    wind_lanes = spaced(0)
    for i in range(TILE):
        block = jnp.where(group == 6, pltpu.roll(wind_lanes, (96 - 16 * i) % 128, 1), 0.0)
        for k in range(KB):
            block = jnp.where(group == k, pltpu.roll(by_lon[k], (16 * (k - i)) % 128, 1), block)
        rows_v[pl.ds(i, MP, stride=TILE), :] = block
    a1_send[...] = rows_v[...].reshape(PLANES, PLANE, TILE, 128).astype(BF16)

    for copy in loads[5:]:
        copy.wait()
    own_level = iota((LEV, OBS), 0) == e
    lane_rows = iota((WIDE, OBS), 0)
    places, observed = [], []
    for t in range(SLOTS):
        lon = lon_v[t]
        block = (lon * 10923) >> 16
        place = lon + 2 * block
        places.append(place)
        weight = wgt_v[t]
        level_rows = []
        for i in range(TILE):
            start = LEV * (TILE * t + i)
            level_rows.append(
                jnp.sum(
                    jnp.where(own_level, inn_v[start : start + LEV, :], 0.0),
                    axis=0, keepdims=True,
                )
            )
        level_innovation = jnp.concatenate(level_rows, axis=0)
        observed.append(level_innovation)
        parts = split3(weight) + split3(weight * level_innovation)
        for i in range(TILE):
            hits = (lane_rows == place[i : i + 1, :]).astype(F32).astype(BF16)
            lhs = jnp.concatenate(
                [part[i : i + 1, :] for part in parts] + [jnp.zeros((2, OBS), F32)], axis=0
            ).astype(BF16)
            sums = lax.dot_general(
                lhs, hits, (((1,), (1,)), ((), ())), preferred_element_type=F32
            )
            half, to = 1 + i // 2, 64 * (i % 2) + 8 * t
            sparse_v[half, to : to + 1, :] = sums[0:1] + sums[1:2] + sums[2:3]
            sparse_v[half, to + 32 : to + 33, :] = sums[3:4] + sums[4:5] + sums[5:6]
    for half in range(2):
        pairs_v[pl.ds(half, MP, stride=2), :] = spaced(1 + half)
    f_send[...] = pairs_v[...].reshape(PLANES, PLANE, 2, 128)
    pl.semaphore_wait(barrier, PLANE + PLANES + ENS - 3)

    def to_plane(src, middle, n):
        for d in LEVEL_ORDER:
            to = (rank + d) % PLANE
            pltpu.make_async_remote_copy(
                src_ref=src.at[:, to], dst_ref=middle.at[rank],
                send_sem=send_sem.at[0], recv_sem=recv_sem.at[n],
                device_id={"mp": plane * PLANE + to}, device_id_type=MESH,
            ).start()
        pltpu.make_async_copy(src.at[:, rank], middle.at[rank], recv_sem.at[n]).start()

    def to_line(middle, dst, n):
        for d in range(1, PLANES):
            to = (plane + d) % PLANES
            pltpu.make_async_remote_copy(
                src_ref=middle.at[:, to], dst_ref=dst.at[plane],
                send_sem=send_sem.at[0], recv_sem=recv_sem.at[n],
                device_id={"mp": to * PLANE + rank}, device_id_type=MESH,
            ).start()
        pltpu.make_async_copy(middle.at[:, plane], dst.at[plane], recv_sem.at[n]).start()

    def line_first(src, middle, n):
        for d in range(1, PLANES):
            to = (plane + d) % PLANES
            pltpu.make_async_remote_copy(
                src_ref=src.at[to], dst_ref=middle.at[plane],
                send_sem=send_sem.at[0], recv_sem=recv_sem.at[n],
                device_id={"mp": to * PLANE + rank}, device_id_type=MESH,
            ).start()
        pltpu.make_async_copy(src.at[plane], middle.at[plane], recv_sem.at[n]).start()

    def plane_next(middle, dst, n):
        def send(d, carry):
            to = (rank + d) % PLANE
            pltpu.make_async_remote_copy(
                src_ref=middle.at[:, to], dst_ref=dst.at[:, rank],
                send_sem=send_sem.at[0], recv_sem=recv_sem.at[n],
                device_id={"mp": plane * PLANE + to}, device_id_type=MESH,
            ).start()
            return carry

        lax.fori_loop(1, PLANE, send, 0)
        pltpu.make_async_copy(middle.at[:, rank], dst.at[:, rank], recv_sem.at[n]).start()

    def to_near(src, dst, slots, n):
        for slot, offset in slots:
            pltpu.make_async_remote_copy(
                src_ref=src, dst_ref=dst.at[slot], send_sem=send_sem.at[0],
                recv_sem=recv_sem.at[n],
                device_id={"mp": (q - offset + MP) % MP}, device_id_type=MESH,
            ).start()

    def arrived(ref, n):
        pltpu.make_async_copy(ref, ref, recv_sem.at[n]).wait()

    def sent(ref, n):
        pltpu.make_async_copy(ref, ref, send_sem.at[0]).wait()

    to_plane(a1_send, a1_mid, 0)
    line_first(f_send, f_mid, 1)

    for copy in loads[1:3]:
        copy.wait()
    band = jnp.concatenate([band_v[...].astype(F32), jnp.ones((1, LATP - LAT), F32)], axis=1)
    width_j = jnp.broadcast_to(band, (LATP, LATP))
    width_i = width_j.T
    row, column = iota((LATP, LATP), 0), iota((LATP, LATP), 1)
    distance = jnp.abs(row - column).astype(F32)
    weights = jnp.maximum(0.0, 1.0 - 2.0 * distance / (width_i + width_j))
    kern_v[...] = jnp.where((row < LAT) & (column < LAT), weights, 0.0).astype(BF16)
    spread = jnp.dot(ctl_v[...], kern_v[0:LAT, :], preferred_element_type=F32)
    spread_v[...] = spread.astype(BF16).astype(F32)


    by_tile = lax.dot_general(
        kern_v[0:LAT, 0:LAT], ctl_v[...], (((1,), (1,)), ((), ())), preferred_element_type=F32
    )
    rows_v[...] = jnp.concatenate([by_tile, jnp.zeros((LAT, 128 - KB * LEV), F32)], axis=1)
    by_row = [rows_v[pl.ds(i, MP, stride=TILE), :] for i in range(TILE)]
    for r in range(TILE - 1):
        block = jnp.zeros((MP, 128), F32)
        for h in range(2):
            k = 2 * r + h
            for i in range(TILE):
                moved = pltpu.roll(by_row[i], (64 * h + 16 * (i - k)) % 128, 1)
                block = jnp.where(group == 4 * h + i, moved, block)
        rows_v[pl.ds(r, MP, stride=TILE), :] = block
    b_send[...] = rows_v[...].reshape(PLANES, PLANE, TILE, 128).astype(BF16)
    line_first(b_send, b_mid, 6)


    arrived(a1_mid, 0)
    to_line(a1_mid, a1_recv, 8)
    arrived(f_mid, 1)
    plane_next(f_mid, f_recv, 9)
    arrived(b_mid, 6)
    plane_next(b_mid, b_recv, 10)
    arrived(a1_recv, 8)
    gathered = a1_recv[...].astype(F32).reshape(LAT, 128)
    ensk = jnp.concatenate([gathered, jnp.zeros((LATP - LAT, 128), F32)], axis=0).T
    ensk_v[...] = ensk[0 : KB * LEV, :]
    part = ensk[0 : KB * LEV, :] * spread_v[...]
    for k in range(KB):
        for h in range(2):
            part_v[pl.ds(8 * h + k, LEV, stride=16), :] = part[
                LEV * k : LEV * (k + 1), 128 * h : 128 * (h + 1)
            ]

    part_s[...] = part_v[...].reshape(LEV, 16, 128).astype(PART)

    def to_levels(src, dst, n):
        for slot, d in enumerate(LEVEL_ORDER):
            to = (e + d) % ENS
            pltpu.make_async_remote_copy(
                src_ref=src.at[to], dst_ref=dst.at[slot],
                send_sem=send_sem.at[0], recv_sem=recv_sem.at[n],
                device_id={"ens": to}, device_id_type=MESH,
            ).start()

    to_levels(part_s, rs_recv, 4)
    fldw_v[...] = ensk[96:112, :]
    fldw_s[...] = ensk[96:112, :].astype(BF16)
    to_near(fldw_s, fldw_recv, ((0, -2), (1, -1), (2, 1), (3, 2)), 3)
    to_near(wind_s, wind_recv, ((0, -1), (1, 1)), 11)

    arrived(f_recv, 9)
    pairs_v[...] = f_recv[...].reshape(2 * MP, 128)
    for half in range(2):
        block = pairs_v[pl.ds(half, MP, stride=2), :]
        rows_v[pl.ds(2 * half, MP, stride=TILE), :] = block
        rows_v[pl.ds(2 * half + 1, MP, stride=TILE), :] = pltpu.roll(block, 64, 1)
    fields = jnp.concatenate([rows_v[...], jnp.zeros((LATP - LAT, 128), F32)], axis=0).T
    fld_v[...] = fields[0:FIELDS, :]
    for t in range(SLOTS):
        n, at = t + 1, t * (t + 1) // 2
        for base, field in ((0, 8 * t), (10, 32 + 8 * t)):
            edge_v[0, base + at : base + at + n, :] = fld_v[field + KB - n : field + KB, :]
            edge_v[1, base + at : base + at + n, :] = fld_v[field : field + n, :]
    for side in range(2):
        fldn_s[side, 0:20, :] = edge_v[side, 0:20, 0:128]
        fldn_s[side, 20:30, :] = edge_v[side, 0:10, 128:256] + pltpu.roll(
            edge_v[side, 10:20, 128:256], 64, 1
        )
    to_near(fldn_s.at[0], fld_near, ((0, -1),), 2)
    to_near(fldn_s.at[1], fld_near, ((1, 1),), 2)
    arrived(b_recv, 10)
    rows_v[...] = b_recv[...].astype(F32).reshape(LAT, 128)
    for r in range(KB // 2):
        block = rows_v[pl.ds(r, MP, stride=TILE), :]
        wide_v[pl.ds(2 * r, MP, stride=8), :] = block
        wide_v[pl.ds(2 * r + 1, MP, stride=8), :] = pltpu.roll(block, 64, 1)
    native = wide_v[...].T
    for i in range(TILE):
        own = ensw_v[LEV * i : LEV * (i + 1), :] * native[LEV * i : LEV * (i + 1), :]
        for c in range(3):
            part2_v[pl.ds(4 * c + i, LEV, stride=16), :] = own[:, 128 * c : 128 * (c + 1)]
    part2_s[...] = part2_v[...].reshape(LEV, 16, 128).astype(PART2)
    to_levels(part2_s, rs2_recv, 12)

    arrived(rs_recv, 4)
    total = part_s[e].astype(F32)
    for d in range(ENS - 1):
        total = total + rs_recv[d].astype(F32)
    inc_v[:, 0:128] = total[0:8]
    inc_v[:, 128:256] = total[8:16]
    inc_far_s[0] = inc_v[4:6, :]
    inc_far_s[1] = inc_v[0:2, :]
    to_near(inc_far_s.at[0], halo_far, ((0, -2),), 14)
    to_near(inc_far_s.at[1], halo_far, ((1, 2),), 14)
    to_near(inc_v, halo_recv, ((0, -1), (1, 1)), 5)
    arrived(rs2_recv, 12)
    total = part2_s[e].astype(F32)
    for d in range(ENS - 1):
        total = total + rs2_recv[d].astype(F32)
    inc2_v[...] = total
    to_near(inc2_v, halo2_recv, ((0, -1), (1, 1)), 13)
    arrived(fld_near, 2)
    arrived(fldw_recv, 3)
    near = [fldw_recv[n].astype(F32) for n in range(4)]
    low_half = iota((10, 128), 1) < 64
    for side in range(2):
        rest = fld_near[side, 20:30, :]
        edge_v[side, 0:20, 0:128] = fld_near[side, 0:20, :]
        edge_v[side, 0:10, 128:256] = jnp.where(low_half, rest, 0.0)
        edge_v[side, 10:20, 128:256] = jnp.where(low_half, pltpu.roll(rest, 64, 1), 0.0)
    inside = (iota((KROWS, LATP), 1) < LAT) & (iota((KROWS, LATP), 0) < 22)
    blank = jnp.zeros((2, LATP), F32)
    winds = []
    for at in (0, 8):
        winds.append(
            jnp.concatenate(
                [
                    near[0][at + 4 : at + 6], near[1][at : at + 6], fldw_v[at : at + 6, :],
                    near[2][at : at + 6], near[3][at : at + 2], blank,
                ],
                axis=0,
            )
        )
    east, north = winds
    coefs = (
        1.0 - jnp.abs(east) - jnp.abs(north),
        jnp.maximum(east, 0.0), jnp.maximum(-east, 0.0),
        jnp.maximum(north, 0.0), jnp.maximum(-north, 0.0),
    )
    for n, coef in enumerate(coefs):
        coef_v[n] = jnp.where(inside, coef, 0.0)
    for t in range(SLOTS):
        n, at = t + 1, t * (t + 1) // 2
        for full, base, field in ((dfull_v, at, 8 * t), (bfull_v, 10 + at, 32 + 8 * t)):
            full[t, 8 - n : 8, :] = edge_v[0, base : base + n, :]
            full[t, 8:14, :] = fld_v[field : field + KB, :]
            full[t, 14 : 14 + n, :] = edge_v[1, base : base + n, :]

    state_v[0, 8:14, :] = inc_v[0:6, :]
    arrived(halo_recv, 5)
    arrived(halo_far, 14)
    state_v[0, 0:2, :] = halo_far[0]
    state_v[0, 2:8, :] = halo_recv[0, 0:6, :]
    state_v[0, 14:20, :] = halo_recv[1, 0:6, :]
    state_v[0, 20:22, :] = halo_far[1]

    def west(value):
        return pltpu.roll(value, 1, 0)

    def east_of(value):
        return pltpu.roll(value, KROWS - 1, 0)

    def below(value):
        return pltpu.roll(value, 1, 1)

    def above(value):
        return pltpu.roll(value, LATP - 1, 1)

    center, from_west, from_east, from_south, from_north = [coef_v[n] for n in range(5)]
    quantity = state_v[0]
    for t in range(SLOTS):
        quantity = (
            center * quantity + from_west * west(quantity) + from_east * east_of(quantity)
            + from_south * below(quantity) + from_north * above(quantity)
        )
        state_v[t] = quantity

    sens = jnp.zeros((KROWS, LATP), F32)
    for t in reversed(range(SLOTS)):
        sens = sens + (dfull_v[t] * state_v[t] - bfull_v[t])
        sens = (
            center * sens + east_of(from_west * sens) + west(from_east * sens)
            + above(from_south * sens) + below(from_north * sens)
        )
    own = jnp.concatenate([sens[8:14, :], jnp.zeros((2, LATP), F32)], axis=0)
    ag_send[...] = own.astype(SENS)

    for d in LEVEL_ORDER:
        pltpu.make_async_remote_copy(
            src_ref=ag_send, dst_ref=ag_recv.at[e],
            send_sem=send_sem.at[0], recv_sem=recv_sem.at[7],
            device_id={"ens": (e + d) % ENS}, device_id_type=MESH,
        ).start()
    pltpu.make_async_copy(ag_send, ag_recv.at[e], recv_sem.at[7]).start()

    arrived(wind_recv, 11)
    row = iota((TROWS, WIDE), 0)
    globe = row + (TILE * q - TILE)
    inside = (globe >= 0) & (globe < LAT) & (row < 12)
    slabs = [wind_recv[0].astype(F32), wind_v[...], wind_recv[1].astype(F32)]
    blank = jnp.zeros((TILE, WIDE), F32)
    east = jnp.concatenate([slab[0:4] for slab in slabs] + [blank], axis=0)
    north = jnp.concatenate([slab[4:8] for slab in slabs] + [blank], axis=0)
    coefs = (
        1.0 - jnp.abs(east) - jnp.abs(north),
        jnp.maximum(east, 0.0), jnp.maximum(-east, 0.0),
        jnp.maximum(north, 0.0), jnp.maximum(-north, 0.0),
    )
    for n, coef in enumerate(coefs):
        coef2_v[n] = jnp.where(inside, coef, 0.0)
    arrived(halo2_recv, 13)
    for s in range(3):
        for c in range(3):
            if s == 1:
                piece = inc2_v[4 * c : 4 * c + 4, :]
            else:
                piece = halo2_recv[s // 2, 4 * c : 4 * c + 4, :]
            state2_v[4 * s : 4 * s + 4, 128 * c : 128 * (c + 1)] = piece
    lane = iota((TROWS, WIDE), 1) & 7
    first, last = lane == 0, lane == KB - 1
    center, from_west, from_east, from_south, from_north = [coef2_v[n] for n in range(5)]
    quantity = jnp.where(inside, state2_v[...], 0.0)
    sampled = []
    for t in range(SLOTS):
        quantity = (
            center * quantity
            + from_west
            * jnp.where(first, pltpu.roll(quantity, 3, 1), pltpu.roll(quantity, 1, 1))
            + from_east
            * jnp.where(
                last, pltpu.roll(quantity, WIDE - 3, 1), pltpu.roll(quantity, WIDE - 1, 1)
            )
            + from_south * pltpu.roll(quantity, 1, 0)
            + from_north * pltpu.roll(quantity, TROWS - 1, 0)
        )
        sampled.append(quantity[4:8, :])
    for h in range(2):
        pair = jnp.concatenate(sampled[2 * h : 2 * h + 2], axis=0)
        place = jnp.concatenate(places[2 * h : 2 * h + 2], axis=0)
        value = jnp.zeros((8, OBS), F32)
        for c in range(3):
            picked = jnp.take_along_axis(pair[:, 128 * c : 128 * (c + 1)], place & 127, axis=1)
            value = jnp.where((place >> 7) == c, picked, value)
        dep_v[8 * h : 8 * h + 8, :] = value - jnp.concatenate(observed[2 * h : 2 * h + 2], axis=0)

    sent(a1_mid.at[pl.ds(0, PLANE - 1)], 0)
    sent(a1_recv.at[pl.ds(0, PLANES - 1)], 8)
    for middle, last_ref, n, m in ((b_mid, b_recv, 6, 10), (f_mid, f_recv, 1, 9)):
        sent(middle.at[pl.ds(0, PLANES - 1)], n)
        sent(last_ref.at[:, pl.ds(0, PLANE - 1)], m)
    for ref, n in (
        (fld_near, 2), (fldw_recv, 3), (rs_recv, 4), (halo_recv, 5), (wind_recv, 11),
        (rs2_recv, 12), (halo2_recv, 13), (halo_far, 14),
    ):
        sent(ref, n)

    arrived(ag_recv, 7)
    level_v[...] = ag_recv[...].astype(F32)
    products = jnp.concatenate(
        [
            (ensk_v[LEV * k : LEV * (k + 1), :] * level_v[:, k, :]).astype(BF16).astype(F32)
            for k in range(KB)
        ],
        axis=0,
    ).astype(BF16)
    smooth = jnp.dot(products, kern_v[...], preferred_element_type=F32)
    grad_v[...] = smooth[:, 0:LAT] + ctl_v[...].astype(F32)

    sent(ag_recv.at[pl.ds(0, ENS - 1)], 7)


def move_out(grad_v, dep_v, grad_hbm, dep_hbm, out_sem):
    copies = [
        pltpu.make_async_copy(grad_v, grad_hbm, out_sem.at[0]),
        pltpu.make_async_copy(dep_v, dep_hbm, out_sem.at[1]),
    ]
    for copy in copies:
        copy.start()
    for copy in copies:
        copy.wait()


def shards(
    ensemble, control, band, wind_east, wind_north, observation_longitude, innovation,
    observation_weight,
):
    operands = (
        ensemble.reshape(TILE * LEV, LON),
        jnp.transpose(control, (1, 3, 2, 0)).reshape(KB * LEV, LAT),
        band.reshape(1, LAT),
        wind_east.reshape(TILE * LEV, LON),
        wind_north.reshape(TILE * LEV, LON),
        observation_longitude,
        innovation.reshape(SLOTS * TILE * LEV, OBS),
        observation_weight,
    )
    operands = tuple(pltpu.with_memory_space_constraint(x, pltpu.HBM) for x in operands)
    anywhere = pl.BlockSpec(memory_space=pl.ANY)
    outs = (
        jax.ShapeDtypeStruct((KB * LEV, LAT), F32),
        jax.ShapeDtypeStruct((SLOTS * TILE, OBS), F32),
    )
    scratch = [pltpu.VMEM(x.shape, x.dtype) for x in operands]
    scratch += [
        pltpu.VMEM((LATP, LATP), BF16),
        pltpu.VMEM((LAT, 128), F32),
        pltpu.VMEM((WIDE, 128), F32),
        pltpu.VMEM((KB * LEV, LATP), F32),
        pltpu.VMEM((KB * LEV, LATP), F32),
        pltpu.VMEM((LON, WIDE), BF16),
        pltpu.VMEM((PLANES, PLANE, TILE, 128), BF16),
        pltpu.VMEM((PLANE, PLANES, TILE, 128), BF16),
        pltpu.VMEM((PLANES, PLANE, TILE, 128), BF16),
        pltpu.VMEM((3, 128, WIDE), F32),
        pltpu.VMEM((PLANES, PLANE, 2, 128), F32),
        pltpu.VMEM((PLANES, PLANE, 2, 128), F32),
        pltpu.VMEM((PLANES, PLANE, 2, 128), F32),
        pltpu.VMEM((FIELDS, LATP), F32),
        pltpu.VMEM((2, 24, LATP), F32),
        pltpu.VMEM((2, 32, 128), F32),
        pltpu.VMEM((2, 32, 128), F32),
        pltpu.VMEM((16, LATP), F32),
        pltpu.VMEM((16, LATP), BF16),
        pltpu.VMEM((4, 16, LATP), BF16),
        pltpu.VMEM((2 * MP, 128), F32),
        pltpu.VMEM((LEV * 16, 128), F32),
        pltpu.VMEM((LEV, 16, 128), PART),
        pltpu.VMEM((ENS - 1, 16, 128), PART),
        pltpu.VMEM((8, LATP), F32),
        pltpu.VMEM((2, 8, LATP), F32),
        pltpu.VMEM((2, 2, LATP), F32),
        pltpu.VMEM((2, 2, LATP), F32),
        pltpu.VMEM((SLOTS, KROWS, LATP), F32),
        pltpu.VMEM((5, KROWS, LATP), F32),
        pltpu.VMEM((SLOTS, KROWS, LATP), F32),
        pltpu.VMEM((SLOTS, KROWS, LATP), F32),
        pltpu.VMEM((8, LATP), SENS),
        pltpu.VMEM((ENS, 8, LATP), SENS),
        pltpu.VMEM((ENS, 8, LATP), F32),
        pltpu.VMEM((TILE * LEV, WIDE), F32),
        pltpu.VMEM((PLANES, PLANE, TILE, 128), BF16),
        pltpu.VMEM((PLANES, PLANE, TILE, 128), BF16),
        pltpu.VMEM((PLANES, PLANE, TILE, 128), BF16),
        pltpu.VMEM((LEV * 16, 128), F32),
        pltpu.VMEM((LEV, 16, 128), PART2),
        pltpu.VMEM((ENS - 1, 16, 128), PART2),
        pltpu.VMEM((16, 128), F32),
        pltpu.VMEM((2, 16, 128), F32),
        pltpu.VMEM((8, WIDE), F32),
        pltpu.VMEM((8, WIDE), BF16),
        pltpu.VMEM((2, 8, WIDE), BF16),
        pltpu.VMEM((TROWS, WIDE), F32),
        pltpu.VMEM((5, TROWS, WIDE), F32),
        pltpu.SemaphoreType.DMA((4,)),
        pltpu.SemaphoreType.DMA((1,)),
        pltpu.SemaphoreType.DMA((15,)),
    ]
    gradient, departures = pl.pallas_call(
        body,
        out_shape=outs,
        in_specs=[anywhere] * len(operands),
        out_specs=(pl.BlockSpec(memory_space=pltpu.VMEM),) * 2,
        scratch_shapes=scratch,
        compiler_params=pltpu.CompilerParams(
            collective_id=0, has_side_effects=True, vmem_limit_bytes=16 * 1024 * 1024
        ),
        name="assimilate",
    )(*operands)
    gradient, departures = pl.pallas_call(
        move_out,
        out_shape=outs,
        in_specs=[anywhere] * 2,
        out_specs=(pl.BlockSpec(memory_space=pltpu.HBM),) * 2,
        scratch_shapes=[pltpu.SemaphoreType.DMA((2,))],
        compiler_params=pltpu.CompilerParams(vmem_limit_bytes=1024 * 1024),
        name="move_out",
    )(gradient, departures)
    gradient = jnp.transpose(gradient.reshape(1, KB, LEV, LAT), (3, 0, 2, 1))
    return gradient, departures.reshape(SLOTS, TILE, 1, OBS)


def solution(mesh):
    placed = (
        P("mp", "ens", None, None),
        P(None, "ens", None, "mp"),
        P(),
        P("mp", None, None),
        P("mp", None, None),
        P(None, "mp", None),
        P(None, "mp", None, None),
        P(None, "mp", None),
    )
    return jax.shard_map(
        shards,
        mesh=mesh,
        in_specs=placed,
        out_specs=(P(None, "ens", None, "mp"), P(None, "mp", "ens", None)),
        check_vma=False,
    )
```
